256 devices in a mesh: depth: 8 (over y, core), lat: 32 (over z, x).
Axes of the slice: x: 4, y: 4, z: 8, core: 2. Of those that a mesh axis runs over, the one named last changes fastest.
Arguments:
- field: float32 [8, 1, 2, 1024, 1024], P('depth', None, None, 'lat'), may hold values from -6 to 6
- fresh: float32 [1, 2, 1024, 1024], P(None, None, 'lat'), may hold values from -6 to 6
- freq_index: int32 [8, 1], P('depth'), may hold values from 0 to 219
- ref_slowness: float32 [8], P('depth'), may hold values from 0.22 to 0.67
- slowness: float32 [8, 1024, 1024], P('depth', 'lat'), may hold values from 0.22 to 0.67
- tile_classes: int32 [8, 32, 32], P('depth', 'lat'), may hold values from 0 to 15
- fd_blocks: float32 [16, 2, 32, 32], replicated, as said below
- fd_coupling: float32 [16, 2], replicated, may hold values from 0.1 to 0.6
- image: float32 [8, 1024, 1024], P('depth', 'lat'), may hold values from -6 to 6
Outputs:
- next_field: float32 [8, 1, 2, 1024, 1024], P('depth', None, None, 'lat')
- new_image: float32 [8, 1024, 1024], P('depth', 'lat')
The draws below stay inside these ranges and needn't reach their ends.
Inputs may be any that keep to these rules, and one draw needn't show every extreme that they name: `fd_blocks`: real and imaginary parts of one complex matrix of order 32 for each of the 16 velocity classes.
All inputs are finite; a program needn't handle non-finite values.
Results may differ from the reference program's by a relative error of at most 0.0003.
Values sent between devices are 32-bit elements; how exact they have to be, the bound alone decides.
No kernel may reach another device: no remote copies, remote signals or barrier semaphores. Data moves between devices by JAX's collectives and lax.ppermute only.
A program may use at most 64 MiB of HBM per device.

```python
import math
import jax
import jax.numpy as jnp
from jax import lax

NX = 1024
NY = 1024
BL = 32
CLASSES = 16
LEVELS = 1
FREQ = 1
NFREQ = 220
SECTIONS = 8
NLEV = 8


def draw_fd_blocks(key, part):
    noise_key, diag_key, skew_key = jax.random.split(key, 3)
    noise = jax.random.normal(noise_key, (CLASSES, 2, BL, BL), jnp.float32)
    spread = 0.45 / math.sqrt(BL)
    indices = jnp.arange(BL, dtype=jnp.int32)
    identity = (indices[:, None] == indices[None, :]).astype(jnp.float32)
    diag_real = jax.random.uniform(diag_key, (CLASSES, BL, 1), jnp.float32, 0.7, 1.3)
    diag_imag = jax.random.uniform(skew_key, (CLASSES, BL, 1), jnp.float32, -0.3, 0.3)
    part_real = noise[:, 0] * spread + identity[None] * diag_real
    part_imag = noise[:, 1] * spread + identity[None] * diag_imag
    return jnp.stack([part_real, part_imag], axis=1)


def touch_ends(entries, stream_key, least, top_value):
    place = [jax.random.randint(jax.random.fold_in(stream_key, axis), (), 0, length) for axis, length in enumerate(entries.shape)]
    longest = entries.shape.index(max(entries.shape))
    neighbour = place[:longest] + [(place[longest] + 1) % entries.shape[longest]] + place[longest + 1:]
    return entries.at[tuple(place)].set(least).at[tuple(neighbour)].set(top_value)


def shard_levels(rng, extent, cuts, smallest, largest):
    def one(position, blocks):
        heights = jax.random.uniform(jax.random.fold_in(jax.random.fold_in(rng, 6), position), (blocks,), jnp.float32, smallest / len(cuts), largest / len(cuts))
        return jnp.repeat(jnp.exp(heights), extent[position] // blocks).reshape((-1,) + (1,) * (len(extent) - position - 1))

    gain = one(*cuts[0])
    for cut in cuts[1:]:
        gain = gain * one(*cut)
    return gain


def gaussian(own_key, dims, scale, most, cuts=(), kind=jnp.bfloat16):
    entries = jax.random.normal(own_key, dims, jnp.float32) * scale
    if len(cuts) > 0:
        entries = shard_levels(own_key, dims, cuts, -0.22, 0.18) * entries
    return jnp.clip(entries, min=-most, max=most).astype(kind)


def setup_inputs(seed: int = 0) -> dict:
    key_list = jax.random.split(jax.random.key(seed), 10)
    field = gaussian(key_list[0], (SECTIONS, FREQ, 2, NX, NY), 1.0, 6.0, ((0, 8), (3, 32)), jnp.float32)
    fresh = gaussian(key_list[1], (FREQ, 2, NX, NY), 1.0, 6.0, ((2, 32),), jnp.float32)
    freq_index = touch_ends(jax.random.randint(key_list[2], (SECTIONS, FREQ), 0, NFREQ), jax.random.fold_in(key_list[2], 1), 0, NFREQ - 1).astype(jnp.int32)
    ref_slowness = jnp.clip(jnp.exp(math.log(0.67) - 1.1136502 * jax.random.uniform(key_list[3], (NLEV,), jnp.float32) ** shard_levels(key_list[3], (NLEV,), ((0, 8),), -0.2, 0.2)), 0.22, 0.67)
    slowness = jnp.clip(jnp.exp(math.log(0.67) - 1.1136502 * jax.random.uniform(key_list[4], (NLEV, NX, NY), jnp.float32) ** shard_levels(key_list[4], (NLEV, NX, NY), ((0, 8), (1, 32)), -0.2, 0.2)), 0.22, 0.67)
    tile_classes = touch_ends(jax.random.randint(key_list[5], (NLEV, NX // BL, NY // BL), 0, CLASSES), jax.random.fold_in(key_list[5], 1), 0, CLASSES - 1).astype(jnp.int32)
    fd_blocks = draw_fd_blocks(jax.random.fold_in(key_list[9], 71), 0)
    fd_coupling = jnp.clip(jax.random.uniform(key_list[7], (CLASSES, 2), jnp.float32, 0.1, 0.6), 0.1, 0.6)
    image = gaussian(key_list[8], (NLEV, NX, NY), 1.0, 6.0, ((0, 8), (1, 32)), jnp.float32)
    return dict(field=field, fresh=fresh, freq_index=freq_index, ref_slowness=ref_slowness, slowness=slowness, tile_classes=tile_classes, fd_blocks=fd_blocks, fd_coupling=fd_coupling, image=image)


LOW_HZ = 5.0
STEP_HZ = 0.25
DEPTH_KM = 0.01
SPACING_KM = 0.025
HIGHEST = lax.Precision.HIGHEST

def wavenumbers(indices, length):
    wrapped = jnp.where(indices < length // 2, indices, indices - length)
    return wrapped.astype(jnp.float32) * (2.0 * math.pi / (length * SPACING_KM))

def propagator(reach, first_k, second_k):
    square = reach * reach - first_k * first_k - second_k * second_k
    root = jnp.sqrt(jnp.abs(square))
    angle = jnp.where(square > 0, root * DEPTH_KM, 0.0)
    amplitude = jnp.where(square > 0, 1.0, jnp.exp(-root * DEPTH_KM))
    return (amplitude * jnp.cos(angle), amplitude * jnp.sin(angle))

def contract(pattern, left, right):
    return jnp.einsum(pattern, left.astype(jnp.float32), right.astype(jnp.float32), precision=HIGHEST)

def fd_step(values, second_diff, coupling, matrices, along_rows, block):
    lead, _, rows, cols = values.shape
    tiles_x = rows // block
    tiles_y = cols // block
    value_tiles = values.reshape(lead, 2, tiles_x, block, tiles_y, block)
    diff_tiles = second_diff.reshape(lead, 2, tiles_x, block, tiles_y, block)
    beta_real = coupling[:, :, 0][:, None, :, None]
    beta_imag = coupling[:, :, 1][:, None, :, None]
    rhs_real = value_tiles[:, 0] + beta_real * diff_tiles[:, 0] - beta_imag * diff_tiles[:, 1]
    rhs_imag = value_tiles[:, 1] + beta_real * diff_tiles[:, 1] + beta_imag * diff_tiles[:, 0]
    if along_rows:
        pattern = 'xyik,gxkyj->gxiyj'
    else:
        pattern = 'xyjk,gxiyk->gxiyj'
    mat_real = matrices[:, :, 0]
    mat_imag = matrices[:, :, 1]
    out_real = contract(pattern, mat_real, rhs_real) - contract(pattern, mat_imag, rhs_imag)
    out_imag = contract(pattern, mat_real, rhs_imag) + contract(pattern, mat_imag, rhs_real)
    return jnp.stack([out_real, out_imag], axis=1).reshape(lead, 2, rows, cols)

def advance_whole(values, omega, reference_slow, slow_level, classes, fd_blocks, fd_coupling, kx_all, ky_all):
    spectrum = jnp.fft.fft2(lax.complex(values[0, 0], values[0, 1]))
    phase_real, phase_imag = propagator(omega * reference_slow, kx_all[:, None], ky_all[None, :])
    spectrum = spectrum * lax.complex(phase_real, phase_imag)
    spatial = jnp.fft.ifft2(spectrum)
    spatial_real = jnp.real(spatial)
    spatial_imag = jnp.imag(spatial)
    angle = omega * (slow_level - reference_slow) * DEPTH_KM
    lens_real = jnp.cos(angle)
    lens_imag = jnp.sin(angle)
    lensed_real = spatial_real * lens_real - spatial_imag * lens_imag
    lensed_imag = spatial_real * lens_imag + spatial_imag * lens_real
    lensed = jnp.stack([lensed_real, lensed_imag], axis=0)[None]
    coupling = jnp.take(fd_coupling, classes, axis=0)
    matrices = jnp.take(fd_blocks, classes, axis=0)
    block = fd_blocks.shape[2]
    padded = jnp.pad(lensed, ((0, 0), (0, 0), (1, 1), (0, 0)))
    diff_x = padded[:, :, 2:] + padded[:, :, :-2] - 2.0 * lensed
    across = fd_step(lensed, diff_x, coupling, matrices, True, block)
    padded_y = jnp.pad(across, ((0, 0), (0, 0), (0, 0), (1, 1)))
    diff_y = padded_y[:, :, :, 2:] + padded_y[:, :, :, :-2] - 2.0 * across
    return fd_step(across, diff_y, coupling, matrices, False, block)

def reference(field, fresh, freq_index, ref_slowness, slowness, tile_classes, fd_blocks, fd_coupling, image):
    kx_all = wavenumbers(jnp.arange(NX, dtype=jnp.int32), NX)
    ky_all = wavenumbers(jnp.arange(NY, dtype=jnp.int32), NY)
    moved = [fresh]
    image_levels = []
    for section_id in range(SECTIONS):
        level_sums = [image[section_id * LEVELS + depth_step] for depth_step in range(LEVELS)]
        slices_out = []
        for slice_id in range(FREQ):
            omega = 2.0 * math.pi * (LOW_HZ + STEP_HZ * freq_index[section_id, slice_id].astype(jnp.float32))
            values = field[section_id, slice_id][None]
            for depth_step in range(LEVELS):
                level_id = section_id * LEVELS + depth_step
                values = advance_whole(values, omega, ref_slowness[level_id], slowness[level_id], tile_classes[level_id], fd_blocks, fd_coupling, kx_all, ky_all)
                level_sums[depth_step] = level_sums[depth_step] + values[0, 0]
            slices_out.append(values[0])
        image_levels.extend(level_sums)
        if section_id + 1 < SECTIONS:
            moved.append(jnp.stack(slices_out, axis=0))
    return (jnp.stack(moved, axis=0), jnp.stack(image_levels, axis=0))
```

```python
import math

import jax
import jax.numpy as jnp
import ml_dtypes
import numpy as np
from jax import lax
from jax.experimental import pallas as pl
from jax.experimental.pallas import tpu as pltpu
from jax.sharding import PartitionSpec as P

LOW_HZ = 5.0
STEP_HZ = 0.25
DEPTH_KM = 0.01
SPACING_KM = 0.025
N = 1024
LAT = 32
NORM = 1.0 / (N * N)
INTERPRET = False


def parts(values):
    high = values.astype(ml_dtypes.bfloat16)
    low = (values - high.astype(np.float64)).astype(ml_dtypes.bfloat16)
    return np.stack([high, low])


def rotation(angle):
    cos, sin = np.cos(angle), np.sin(angle)
    return np.stack([np.stack([cos, -sin]), np.stack([sin, cos])])


def tables():
    n2 = np.arange(128)
    small = np.arange(32)
    k2 = np.arange(128).reshape(32, 4)
    line = rotation(-2 * np.pi * (k2[:, :, None] * n2 % 128) / 128)
    w1 = line.transpose(2, 0, 3, 1, 4).reshape(256, 256)
    line = rotation(2 * np.pi * (k2[:, :, None] * n2 % 128) / 128)
    w3 = line.transpose(2, 1, 3, 0, 4).reshape(256, 256)
    grid = 2 * np.pi * (small[:, None] * small % 32) / 32
    eye4 = np.eye(4)
    a1 = np.einsum("dcqi,kl->dkqicl", rotation(-grid), eye4).reshape(256, 256)
    a2 = np.einsum("dciq,kl->idkclq", rotation(grid), eye4).reshape(256, 256)
    b1 = np.einsum("dcxp,kl->ckxdlp", rotation(-grid), eye4).reshape(256, 256)
    b2 = np.einsum("dcpx,kl->ckpdlx", rotation(grid), eye4).reshape(256, 256)
    ty = 2 * np.pi * np.arange(8)[:, None] * n2 / N
    tx = np.tile(2 * np.pi * small[:, None] * small / N, (1, 4))
    twist_y = np.stack([np.cos(ty), np.sin(ty)]).astype(np.float32)
    twist_x = np.stack([np.cos(tx), np.sin(tx)]).astype(np.float32)
    edge = np.zeros((8, 32, 16, 8))
    for k1 in range(8):
        edge[k1, 31, k1, 0] = 1
        edge[k1, 0, k1, 1] = 1
    edge = edge.reshape(256, 128).astype(ml_dtypes.bfloat16)
    own = (np.arange(128)[None, :] // 32 == np.arange(4)[:, None]).astype(np.float32)
    own = np.broadcast_to(own[:, None, :], (4, 32, 128)).astype(ml_dtypes.bfloat16)
    spread = np.tile(np.eye(32), (1, 4)).astype(ml_dtypes.bfloat16)
    return {
        "w1": parts(w1),
        "w3": parts(w3),
        "a1": parts(a1),
        "a2": parts(a2),
        "b1": parts(b1),
        "b2": parts(b2),
        "twist_y": twist_y,
        "twist_x": twist_x,
        "edge": edge,
        "own": own,
        "spread": spread,
    }


NN = (((1,), (0,)), ((), ()))
NT = (((1,), (1,)), ((), ()))


def split(values):
    high = values.astype(jnp.bfloat16)
    low = (values - high.astype(jnp.float32)).astype(jnp.bfloat16)
    return high, low


def product(left, right, dims=NN):
    dot = lambda a, b: lax.dot_general(a, b, dims, preferred_element_type=jnp.float32)
    return dot(left[0], right[0]) + (dot(left[1], right[0]) + dot(left[0], right[1]))


def cmul(a, b):
    return a[0] * b[0] - a[1] * b[1], a[0] * b[1] + a[1] * b[0]


def dft(values, sign):
    count = len(values)
    if count == 1:
        return values
    even, odd = dft(values[0::2], sign), dft(values[1::2], sign)
    first, second = [], []
    for k in range(count // 2):
        re, im = odd[k]
        if 4 * k == count:
            re, im = -sign * im, sign * re
        elif k:
            cos = math.cos(2 * math.pi * k / count)
            sin = sign * math.sin(2 * math.pi * k / count)
            if 8 * k == count:
                re, im = cos * (re - sign * im), cos * (im + sign * re)
            else:
                re, im = cmul(odd[k], (cos, sin))
        first.append((even[k][0] + re, even[k][1] + im))
        second.append((even[k][0] - re, even[k][1] - im))
    return first + second


def call(body, outs, scratch, args, spaces, flops=0):
    size = sum(math.prod(o.shape) * o.dtype.itemsize for o in outs)
    size += sum(math.prod(a.shape) * a.dtype.itemsize for a in args)
    in_specs = [
        pl.BlockSpec(memory_space=pltpu.SMEM if i in spaces else pltpu.VMEM) for i in range(len(args))
    ]
    return pl.pallas_call(
        body,
        out_shape=outs,
        in_specs=in_specs,
        out_specs=[pl.BlockSpec(memory_space=pltpu.VMEM) for _ in outs],
        scratch_shapes=scratch,
        compiler_params=pltpu.CompilerParams(vmem_limit_bytes=24 << 20),
        cost_estimate=pl.CostEstimate(flops=flops, bytes_accessed=size, transcendentals=0),
        interpret=INTERPRET,
    )(*args)


def shape(*dims, dtype=jnp.float32):
    return jax.ShapeDtypeStruct(dims, dtype)


def forward_y(field_ref, w1_ref, twist_ref, out_ref, high_ref, low_ref):
    for top in range(0, 32, 16):
        rows = slice(top, top + 16)
        lines = [
            tuple(field_ref[c, rows, n1 * 128 : n1 * 128 + 128] for c in range(2)) for n1 in range(8)
        ]
        for k1, value in enumerate(dft(lines, -1)):
            if k1:
                cos, sin = twist_ref[0, k1 : k1 + 1], twist_ref[1, k1 : k1 + 1]
                value = cmul(value, (cos, -sin))
            at = slice(k1 * 32 + top, k1 * 32 + top + 16)
            for c in range(2):
                high, low = split(value[c])
                high_ref[at, c * 128 : c * 128 + 128] = high
                low_ref[at, c * 128 : c * 128 + 128] = low
    out = product((w1_ref[0], w1_ref[1]), (high_ref[...], low_ref[...]), NT)
    out_ref[...] = out.reshape(32, 8, 256)


def sincos(angle):
    return jnp.cos(angle), jnp.sin(angle)


def phases(freq_ref, slow_ref, lat_ref, out_ref):
    omega = 2.0 * math.pi * (LOW_HZ + STEP_HZ * freq_ref[0].astype(jnp.float32))
    reach = omega * slow_ref[0]
    scale = 2.0 * math.pi / (N * SPACING_KM)
    for block in range(8):
        h, k2l = block // 4, block % 4
        q = lax.broadcasted_iota(jnp.int32, (32, 128), 0)
        lane = lax.broadcasted_iota(jnp.int32, (32, 128), 1)
        kx = q + 32 * (lane % 32)
        ky = h * 4 + lane // 32 + 8 * (4 * lat_ref[0] + k2l)
        kx = jnp.where(kx < N // 2, kx, kx - N).astype(jnp.float32) * scale
        ky = jnp.where(ky < N // 2, ky, ky - N).astype(jnp.float32) * scale
        square = reach * reach - kx * kx - ky * ky
        root = jnp.sqrt(jnp.abs(square))
        angle = jnp.where(square > 0, root * DEPTH_KM, 0.0)
        amplitude = jnp.where(square > 0, 1.0, jnp.exp(-root * DEPTH_KM))
        cos, sin = sincos(angle)
        out_ref[0, block * 32 : block * 32 + 32] = amplitude * cos
        out_ref[1, block * 32 : block * 32 + 32] = amplitude * sin


def along_x(in_ref, phase_ref, a1_ref, b1_ref, b2_ref, a2_ref, twist_ref, edge_ref, out_ref, high_ref, low_ref):
    lines = in_ref[...].reshape(256, 256)
    mixed = product((a1_ref[0], a1_ref[1]), split(lines))
    cos, sin = twist_ref[0], twist_ref[1]

    def put(at, value):
        for c in range(2):
            high, low = split(value[c])
            high_ref[at, c * 128 : c * 128 + 128] = high
            low_ref[at, c * 128 : c * 128 + 128] = low

    for h in range(2):
        lanes = slice(h * 128, h * 128 + 128)
        for k2l in range(4):
            value = (mixed[k2l * 32 : k2l * 32 + 32, lanes], mixed[128 + k2l * 32 : 160 + k2l * 32, lanes])
            top = (h * 4 + k2l) * 32
            put(slice(top, top + 32), cmul(value, (cos, -sin)))
    spectrum = product((high_ref[...], low_ref[...]), (b1_ref[0], b1_ref[1]))
    for block in range(8):
        rows = slice(block * 32, block * 32 + 32)
        value = (spectrum[rows, :128], spectrum[rows, 128:])
        put(rows, cmul(value, (phase_ref[0, rows], phase_ref[1, rows])))
    mixed = product((high_ref[...], low_ref[...]), (b2_ref[0], b2_ref[1]))
    for h in range(2):
        for k2l in range(4):
            rows = slice((h * 4 + k2l) * 32, (h * 4 + k2l) * 32 + 32)
            value = cmul((mixed[rows, :128], mixed[rows, 128:]), (cos, sin))
            for c in range(2):
                high, low = split(value[c])
                at = slice(c * 128 + k2l * 32, c * 128 + k2l * 32 + 32)
                high_ref[at, h * 128 : h * 128 + 128] = high
                low_ref[at, h * 128 : h * 128 + 128] = low
    out = product((a2_ref[0], a2_ref[1]), (high_ref[...], low_ref[...]))
    high, low = split(out)
    dot = lambda a: lax.dot_general(a, edge_ref[...], NN, preferred_element_type=jnp.float32)
    edge = (dot(high) + dot(low)).reshape(32, 8, 128)
    out_ref[:, :, :256] = out.reshape(32, 8, 256)
    side = lax.broadcasted_iota(jnp.int32, (32, 8, 128), 2) % 8
    zero = jnp.zeros((1, 8, 128), jnp.float32)
    before = jnp.concatenate([zero, edge[:-1]], axis=0)
    after = jnp.concatenate([edge[1:], zero], axis=0)
    out_ref[:, :, 256:] = jnp.where(side == 0, before, after)


def weights(
    freq_ref, refslow_ref, class_ref, coupling_ref, slow_ref, up_ref, down_ref, blocks_ref, own_ref, spread_ref,
    lens_ref, beta_ref, mx_ref, my_ref, wide_ref,
):
    omega = 2.0 * math.pi * (LOW_HZ + STEP_HZ * freq_ref[0].astype(jnp.float32))
    base = refslow_ref[0]

    def lens(values):
        cos, sin = sincos(omega * (values - base) * DEPTH_KM)
        return cos * NORM, sin * NORM

    for top in range(0, 32, 8):
        lens_ref[0, top : top + 8], lens_ref[1, top : top + 8] = lens(slow_ref[top : top + 8])
    row = lax.broadcasted_iota(jnp.int32, (8, N), 0)
    sides = jnp.where(row == 0, up_ref[...], down_ref[...])
    lens_ref[0, 32:40], lens_ref[1, 32:40] = lens(sides)
    high, low = split(blocks_ref[...])
    dot = lambda a: lax.dot_general(a, spread_ref[...], NN, preferred_element_type=jnp.float32)
    wide_ref[0] = dot(high).astype(jnp.bfloat16).reshape(16, 64, 128)
    wide_ref[1] = dot(low).astype(jnp.bfloat16).reshape(16, 64, 128)
    lane = lax.broadcasted_iota(jnp.int32, (8, 128), 1) // 32
    for g in range(8):
        classes = [class_ref[g * 4 + t] for t in range(4)]
        for c in range(2):
            beta = jnp.full((8, 128), coupling_ref[classes[0] * 2 + c])
            for t in range(1, 4):
                beta = jnp.where(lane == t, coupling_ref[classes[t] * 2 + c], beta)
            beta_ref[c, :, g * 128 : g * 128 + 128] = beta
        for part in range(2):
            total = [None, None]
            for t in range(4):
                for c in range(2):
                    tile = wide_ref[part, classes[t], c * 32 : c * 32 + 32] * own_ref[t]
                    total[c] = tile if t == 0 else total[c] + tile
                    if c == 0:
                        my_ref[part, g, t * 32 : t * 32 + 32, :128] = tile
                        my_ref[part, g, 128 + t * 32 : 160 + t * 32, 128:] = tile
                    else:
                        my_ref[part, g, 128 + t * 32 : 160 + t * 32, :128] = tile
                        my_ref[part, g, t * 32 : t * 32 + 32, 128:] = -tile
            mx_ref[part, g, :32, :128] = total[0]
            mx_ref[part, g, :32, 128:] = -total[1]
            mx_ref[part, g, 32:, :128] = total[1]
            mx_ref[part, g, 32:, 128:] = total[0]


def finish(
    in_ref, w3_ref, twist_ref, lens_ref, beta_ref, mx_ref, my_ref, own_ref, image_ref,
    out_ref, image_out_ref, mixed_ref, lensed_ref, rhs_ref, across_ref,
):
    turned = in_ref[...].reshape(256, 384)[:, :384].T
    mixed_ref[...] = product(split(turned[:320]), (w3_ref[0], w3_ref[1]))
    for block in range(5):
        values = []
        for k1 in range(8):
            top = k1 * 32 + block * 8 if block < 4 else 256 + k1 * 8
            value = (mixed_ref[top : top + 8, :128], mixed_ref[top : top + 8, 128:])
            if k1:
                value = cmul(value, (twist_ref[0, k1 : k1 + 1], twist_ref[1, k1 : k1 + 1]))
            values.append(value)
        for n1, value in enumerate(dft(values, 1)):
            lanes = slice(n1 * 128, n1 * 128 + 128)
            rows = slice(block * 8, block * 8 + 8)
            value = cmul(value, (lens_ref[0, rows, lanes], lens_ref[1, rows, lanes]))
            for c in range(2):
                if block < 4:
                    lensed_ref[c, 8 + block * 8 : 16 + block * 8, lanes] = value[c]
                else:
                    lensed_ref[c, 7:8, lanes] = value[c][0:1]
                    lensed_ref[c, 40:41, lanes] = value[c][1:2]
    for g in range(8):
        lanes = slice(g * 128, g * 128 + 128)
        beta = (beta_ref[0, 0:1, lanes], beta_ref[1, 0:1, lanes])
        mid = [lensed_ref[c, 8:40, lanes] for c in range(2)]
        diff = tuple(
            lensed_ref[c, 9:41, lanes] + lensed_ref[c, 7:39, lanes] - 2.0 * mid[c] for c in range(2)
        )
        more = cmul(diff, beta)
        pieces = [split(mid[c] + more[c]) for c in range(2)]
        rhs = [
            jnp.concatenate([pieces[c][part] * own_ref[t] for c in range(2) for t in range(4)], axis=0)
            for part in range(2)
        ]
        out = product((mx_ref[0, g], mx_ref[1, g]), rhs)
        across_ref[0, :, lanes] = out[:32]
        across_ref[1, :, lanes] = out[32:]
    lane = lax.broadcasted_iota(jnp.int32, (32, N), 1)
    diff = []
    for c in range(2):
        whole = across_ref[c]
        after = jnp.where(lane == N - 1, 0.0, pltpu.roll(whole, N - 1, 1))
        before = jnp.where(lane == 0, 0.0, pltpu.roll(whole, 1, 1))
        diff.append(after + before - 2.0 * whole)
    more = cmul(diff, (beta_ref[0, 0:1], beta_ref[1, 0:1]))
    for c in range(2):
        rhs_ref[c] = across_ref[c] + more[c]
    for g in range(8):
        lanes = slice(g * 128, g * 128 + 128)
        rhs = jnp.concatenate([rhs_ref[0, :, lanes], rhs_ref[1, :, lanes]], axis=1)
        out = product(split(rhs), (my_ref[0, g], my_ref[1, g]), NT)
        out_ref[0, :, lanes] = out[:, :128]
        out_ref[1, :, lanes] = out[:, 128:]
        image_out_ref[:, lanes] = image_ref[:, lanes] + out[:, :128]


def spread_y(field, t):
    scratch = [pltpu.VMEM((256, 256), jnp.bfloat16)] * 2
    return call(forward_y, [shape(32, 8, 256)], scratch, [field, t["w1"], t["twist_y"]], ())[0]


def phase_tables(freq, refslow, lat):
    return call(phases, [shape(2, 256, 128)], [], [freq, refslow, lat], (0, 1, 2))[0]


def continue_x(block, phase, t):
    scratch = [pltpu.VMEM((256, 256), jnp.bfloat16)] * 2
    args = [block, phase, t["a1"], t["b1"], t["b2"], t["a2"], t["twist_x"], t["edge"]]
    return call(along_x, [shape(32, 8, 384)], scratch, args, ())[0]


def correction_tables(freq, refslow, classes, coupling, slow, up, down, blocks, t):
    half = jnp.bfloat16
    outs = [shape(2, 40, N), shape(2, 8, N), shape(2, 8, 64, 256, dtype=half), shape(2, 8, 256, 256, dtype=half)]
    scratch = [pltpu.VMEM((2, 16, 64, 128), half)]
    args = [freq, refslow, classes, coupling, slow, up, down, blocks, t["own"], t["spread"]]
    return call(weights, outs, scratch, args, (0, 1, 2, 3))


def correct(block, tabs, image, t):
    lens, beta, mx, my = tabs
    scratch = [
        pltpu.VMEM((320, 256), jnp.float32),
        pltpu.VMEM((2, 48, N), jnp.float32),
        pltpu.VMEM((2, 32, N), jnp.float32),
        pltpu.VMEM((2, 32, N), jnp.float32),
    ]
    args = [block, t["w3"], t["twist_y"], lens, beta, mx, my, t["own"], image]
    return call(finish, [shape(2, 32, N), shape(32, N)], scratch, args, ())


def exchange(block):
    return lax.all_to_all(block, "lat", split_axis=0, concat_axis=0, tiled=True)


def after(value, *others):
    return lax.optimization_barrier((value, others))


def per_device(
    field, fresh, freq_index, ref_slowness, slowness, tile_classes, fd_blocks, fd_coupling, image
):
    t = tables()
    block = spread_y(field.reshape(2, 32, N), t)
    block, (freq, refslow, slow) = after(block, freq_index.reshape(1), ref_slowness, slowness[0])
    received = exchange(block)
    lat = lax.axis_index("lat").reshape(1).astype(jnp.int32)
    phase = phase_tables(freq, refslow, lat)
    down = lax.ppermute(slow[:1], "lat", [(i + 1, i) for i in range(LAT - 1)])
    up = lax.ppermute(slow[-1:], "lat", [(i, i + 1) for i in range(LAT - 1)])
    block = continue_x(received, phase, t)
    block, (freq, classes, up, down) = after(block, freq, tile_classes.reshape(32), up, down)
    received = exchange(block)
    tabs = correction_tables(
        freq, refslow, classes, fd_coupling.reshape(32), slow, up, down, fd_blocks.reshape(1024, 32), t
    )
    result, new_image = correct(received, tabs, image[0], t)
    count = lax.axis_size("depth")
    moved = lax.ppermute(result, "depth", [(i, i + 1) for i in range(count - 1)])
    first_section = lax.axis_index("depth") == 0
    next_field = jnp.where(first_section, fresh[0], moved)[None, None]
    return next_field, new_image[None]


def solution(mesh):
    return jax.shard_map(
        per_device,
        mesh=mesh,
        in_specs=(
            P("depth", None, None, "lat", None),
            P(None, None, "lat", None),
            P("depth", None),
            P("depth"),
            P("depth", "lat", None),
            P("depth", "lat", None),
            P(),
            P(),
            P("depth", "lat", None),
        ),
        out_specs=(P("depth", None, None, "lat", None), P("depth", "lat", None)),
        check_vma=False,
    )
```

```python
import math

import jax
import jax.numpy as jnp
import ml_dtypes
import numpy as np
from jax import lax
from jax.experimental import pallas as pl
from jax.experimental.pallas import tpu as pltpu
from jax.sharding import PartitionSpec as P

LOW_HZ = 5.0
STEP_HZ = 0.25
DEPTH_KM = 0.01
SPACING_KM = 0.025
N = 1024
LAT = 32
NORM = 1.0 / (N * N)
INTERPRET = False


def parts(values):
    high = values.astype(ml_dtypes.bfloat16)
    low = (values - high.astype(np.float64)).astype(ml_dtypes.bfloat16)
    return np.stack([high, low])


def rotation(angle):
    cos, sin = np.cos(angle), np.sin(angle)
    return np.stack([np.stack([cos, -sin]), np.stack([sin, cos])])


def tables():
    n2 = np.arange(128)
    small = np.arange(32)
    k2 = np.arange(128).reshape(32, 4)
    line = rotation(-2 * np.pi * (k2[:, :, None] * n2 % 128) / 128)
    w1 = line.transpose(2, 0, 3, 1, 4).reshape(256, 256)
    line = rotation(2 * np.pi * (k2[:, :, None] * n2 % 128) / 128)
    w3 = line.transpose(2, 1, 3, 0, 4).reshape(256, 256)
    grid = 2 * np.pi * (small[:, None] * small % 32) / 32
    eye4 = np.eye(4)
    a1 = np.einsum("dcqi,kl->dkqicl", rotation(-grid), eye4).reshape(256, 256)
    a2 = np.einsum("dciq,kl->idkclq", rotation(grid), eye4).reshape(256, 256)
    b1 = np.einsum("dcxp,kl->ckxdlp", rotation(-grid), eye4).reshape(256, 256)
    b2 = np.einsum("dcpx,kl->ckpdlx", rotation(grid), eye4).reshape(256, 256)
    ty = 2 * np.pi * np.arange(8)[:, None] * n2 / N
    tx = np.tile(2 * np.pi * small[:, None] * small / N, (1, 4))
    twist_y = np.stack([np.cos(ty), np.sin(ty)]).astype(np.float32)
    twist_x = np.stack([np.cos(tx), np.sin(tx)]).astype(np.float32)
    edge = np.zeros((8, 32, 16, 8))
    for k1 in range(8):
        edge[k1, 31, k1, 0] = 1
        edge[k1, 0, k1, 1] = 1
    edge = edge.reshape(256, 128).astype(ml_dtypes.bfloat16)
    own = (np.arange(128)[None, :] // 32 == np.arange(4)[:, None]).astype(np.float32)
    own = np.broadcast_to(np.tile(own, (1, 2))[:, None, :], (4, 32, 256)).astype(ml_dtypes.bfloat16)
    spread = np.tile(np.eye(32), (1, 4)).astype(ml_dtypes.bfloat16)
    return {
        "w1": parts(w1),
        "w3": parts(w3),
        "x": np.stack([parts(a1), parts(b1), parts(b2), parts(a2)]),
        "twist_y": twist_y,
        "twist_x": twist_x,
        "edge": edge,
        "own": own,
        "spread": spread,
    }


NN = (((1,), (0,)), ((), ()))
NT = (((1,), (1,)), ((), ()))


def split(values):
    high = values.astype(jnp.bfloat16)
    low = (values - high.astype(jnp.float32)).astype(jnp.bfloat16)
    return high, low


def product(left, right, dims=NN):
    dot = lambda a, b: lax.dot_general(a, b, dims, preferred_element_type=jnp.float32)
    return dot(left[0], right[0]) + (dot(left[1], right[0]) + dot(left[0], right[1]))


def cmul(a, b):
    return a[0] * b[0] - a[1] * b[1], a[0] * b[1] + a[1] * b[0]


def dft(values, sign):
    count = len(values)
    if count == 1:
        return values
    even, odd = dft(values[0::2], sign), dft(values[1::2], sign)
    first, second = [], []
    for k in range(count // 2):
        re, im = odd[k]
        if 4 * k == count:
            re, im = -sign * im, sign * re
        elif k:
            cos = math.cos(2 * math.pi * k / count)
            sin = sign * math.sin(2 * math.pi * k / count)
            if 8 * k == count:
                re, im = cos * (re - sign * im), cos * (im + sign * re)
            else:
                re, im = cmul(odd[k], (cos, sin))
        first.append((even[k][0] + re, even[k][1] + im))
        second.append((even[k][0] - re, even[k][1] - im))
    return first + second


def call(body, outs, scratch, args, scalars=(), large=()):
    size = sum(math.prod(o.shape) * o.dtype.itemsize for o in outs)
    size += sum(math.prod(a.shape) * a.dtype.itemsize for a in args)
    args = [pltpu.with_memory_space_constraint(a, pltpu.HBM) if i in large else a for i, a in enumerate(args)]
    space = lambda i: pltpu.SMEM if i in scalars else pltpu.HBM if i in large else pltpu.VMEM
    return pl.pallas_call(
        body,
        out_shape=outs,
        in_specs=[pl.BlockSpec(memory_space=space(i)) for i in range(len(args))],
        out_specs=[pl.BlockSpec(memory_space=pltpu.VMEM) for _ in outs],
        scratch_shapes=scratch,
        compiler_params=pltpu.CompilerParams(vmem_limit_bytes=24 << 20),
        cost_estimate=pl.CostEstimate(flops=0, bytes_accessed=size, transcendentals=0),
        interpret=INTERPRET,
    )(*args)


def fetch(sources, targets, sems):
    copies = [pltpu.make_async_copy(a, b, sems.at[i]) for i, (a, b) in enumerate(zip(sources, targets, strict=True))]
    for copy in copies:
        copy.start()
    return copies


def shape(*dims, dtype=jnp.float32):
    return jax.ShapeDtypeStruct(dims, dtype)


def forward_y(field_any, twist_any, w1_any, out_ref, field_ref, twist_ref, w1_ref, high_ref, low_ref, sems):
    copies = fetch([field_any, twist_any, w1_any], [field_ref, twist_ref, w1_ref], sems)
    copies[0].wait()
    copies[1].wait()
    for top in range(0, 32, 16):
        rows = slice(top, top + 16)
        lines = [
            tuple(field_ref[c, rows, n1 * 128 : n1 * 128 + 128] for c in range(2)) for n1 in range(8)
        ]
        for k1, value in enumerate(dft(lines, -1)):
            if k1:
                cos, sin = twist_ref[0, k1 : k1 + 1], twist_ref[1, k1 : k1 + 1]
                value = cmul(value, (cos, -sin))
            at = slice(k1 * 32 + top, k1 * 32 + top + 16)
            for c in range(2):
                high, low = split(value[c])
                high_ref[at, c * 128 : c * 128 + 128] = high
                low_ref[at, c * 128 : c * 128 + 128] = low
    copies[2].wait()
    out = product((w1_ref[0], w1_ref[1]), (high_ref[...], low_ref[...]), NT)
    out_ref[...] = out.reshape(32, 8, 256)


def sincos(angle):
    return jnp.cos(angle), jnp.sin(angle)


def phases(freq_ref, slow_ref, lat_ref, x_any, twist_any, edge_any, out_ref, x_ref, twist_ref, edge_ref, sems):
    copies = fetch([x_any, twist_any, edge_any], [x_ref, twist_ref, edge_ref], sems)
    omega = 2.0 * math.pi * (LOW_HZ + STEP_HZ * freq_ref[0].astype(jnp.float32))
    reach = omega * slow_ref[0]
    scale = 2.0 * math.pi / (N * SPACING_KM)
    for block in range(8):
        h, k2l = block // 4, block % 4
        q = lax.broadcasted_iota(jnp.int32, (32, 128), 0)
        lane = lax.broadcasted_iota(jnp.int32, (32, 128), 1)
        kx = q + 32 * (lane % 32)
        ky = h * 4 + lane // 32 + 8 * (4 * lat_ref[0] + k2l)
        kx = jnp.where(kx < N // 2, kx, kx - N).astype(jnp.float32) * scale
        ky = jnp.where(ky < N // 2, ky, ky - N).astype(jnp.float32) * scale
        square = reach * reach - kx * kx - ky * ky
        root = jnp.sqrt(jnp.abs(square))
        angle = jnp.where(square > 0, root * DEPTH_KM, 0.0)
        amplitude = jnp.where(square > 0, 1.0, jnp.exp(-root * DEPTH_KM))
        cos, sin = sincos(angle)
        out_ref[0, block * 32 : block * 32 + 32] = amplitude * cos
        out_ref[1, block * 32 : block * 32 + 32] = amplitude * sin
    for copy in copies:
        copy.wait()


def along_x(in_ref, phase_ref, x_ref, twist_ref, edge_ref, out_ref, high_ref, low_ref):
    lines = in_ref[...].reshape(256, 256)
    mixed = product((x_ref[0, 0], x_ref[0, 1]), split(lines))
    cos, sin = twist_ref[0], twist_ref[1]

    def put(at, value):
        for c in range(2):
            high, low = split(value[c])
            high_ref[at, c * 128 : c * 128 + 128] = high
            low_ref[at, c * 128 : c * 128 + 128] = low

    for h in range(2):
        lanes = slice(h * 128, h * 128 + 128)
        for k2l in range(4):
            value = (mixed[k2l * 32 : k2l * 32 + 32, lanes], mixed[128 + k2l * 32 : 160 + k2l * 32, lanes])
            top = (h * 4 + k2l) * 32
            put(slice(top, top + 32), cmul(value, (cos, -sin)))
    spectrum = product((high_ref[...], low_ref[...]), (x_ref[1, 0], x_ref[1, 1]))
    for block in range(8):
        rows = slice(block * 32, block * 32 + 32)
        value = (spectrum[rows, :128], spectrum[rows, 128:])
        put(rows, cmul(value, (phase_ref[0, rows], phase_ref[1, rows])))
    mixed = product((high_ref[...], low_ref[...]), (x_ref[2, 0], x_ref[2, 1]))
    for h in range(2):
        for k2l in range(4):
            rows = slice((h * 4 + k2l) * 32, (h * 4 + k2l) * 32 + 32)
            value = cmul((mixed[rows, :128], mixed[rows, 128:]), (cos, sin))
            for c in range(2):
                high, low = split(value[c])
                at = slice(c * 128 + k2l * 32, c * 128 + k2l * 32 + 32)
                high_ref[at, h * 128 : h * 128 + 128] = high
                low_ref[at, h * 128 : h * 128 + 128] = low
    out = product((x_ref[3, 0], x_ref[3, 1]), (high_ref[...], low_ref[...]))
    high, low = split(out)
    dot = lambda a: lax.dot_general(a, edge_ref[...], NN, preferred_element_type=jnp.float32)
    edge = (dot(high) + dot(low)).reshape(32, 8, 128)
    out_ref[:, :, :256] = out.reshape(32, 8, 256)
    side = lax.broadcasted_iota(jnp.int32, (32, 8, 128), 2) % 8
    zero = jnp.zeros((1, 8, 128), jnp.float32)
    before = jnp.concatenate([zero, edge[:-1]], axis=0)
    after = jnp.concatenate([edge[1:], zero], axis=0)
    out_ref[:, :, 256:] = jnp.where(side == 0, before, after)


def weights(
    freq_ref, refslow_ref, class_ref, coupling_ref, last_ref, slow_ref, blocks_ref, own_ref, spread_ref,
    lens_ref, row_ref, mx_ref, wide_ref,
):
    omega = 2.0 * math.pi * (LOW_HZ + STEP_HZ * freq_ref[0].astype(jnp.float32))
    base = refslow_ref[0]
    for top in range(0, 32, 8):
        rows = slice(top, top + 8)
        cos, sin = sincos(omega * (slow_ref[rows] - base) * DEPTH_KM)
        lens_ref[0, rows], lens_ref[1, rows] = cos * NORM, sin * NORM
    high, low = split(blocks_ref[...])
    dot = lambda a: lax.dot_general(a, spread_ref[...], NN, preferred_element_type=jnp.float32)
    wide_ref[0] = dot(high).astype(jnp.bfloat16).reshape(16, 64, 128)
    wide_ref[1] = dot(low).astype(jnp.bfloat16).reshape(16, 64, 128)
    row_ref[2:3] = jnp.full((1, N), omega)
    row_ref[3:4] = jnp.full((1, N), base)
    row_ref[4:5] = jnp.full((1, N), last_ref[0].astype(jnp.float32))
    lane = lax.broadcasted_iota(jnp.int32, (1, 128), 1) // 32
    for g in range(8):
        classes = [class_ref[g * 4 + t] for t in range(4)]
        for c in range(2):
            beta = jnp.full((1, 128), coupling_ref[classes[0] * 2 + c])
            for t in range(1, 4):
                beta = jnp.where(lane == t, coupling_ref[classes[t] * 2 + c], beta)
            row_ref[c : c + 1, g * 128 : g * 128 + 128] = beta
        for part in range(2):
            total = []
            for c in range(2):
                tiles = [wide_ref[part, classes[t], c * 32 : c * 32 + 32] * own_ref[t, :, :128] for t in range(4)]
                total.append((tiles[0] + tiles[1]) + (tiles[2] + tiles[3]))
            mx_ref[part, g, :32, :128] = total[0]
            mx_ref[part, g, :32, 128:] = -total[1]
            mx_ref[part, g, 32:, :128] = total[1]
            mx_ref[part, g, 32:, 128:] = total[0]


def finish(
    in_ref, w3_ref, twist_ref, lens_ref, row_ref, mx_ref, own_ref, up_ref, down_ref, fresh_any,
    out_ref, real_ref, mixed_ref, lensed_ref, rhs_ref, across_ref, fresh_ref, sem,
):
    copy = pltpu.make_async_copy(fresh_any, fresh_ref, sem)
    copy.start()
    side = lax.broadcasted_iota(jnp.int32, (8, N), 0)
    sides = jnp.where(side == 0, up_ref[...], down_ref[...])
    cos, sin = sincos(row_ref[2:3] * (sides - row_ref[3:4]) * DEPTH_KM)
    side_lens = cos * NORM, sin * NORM
    turned = in_ref[...].reshape(256, 384)[:, :384].T
    mixed_ref[...] = product(split(turned[:320]), (w3_ref[0], w3_ref[1]))
    for block in range(5):
        values = []
        for k1 in range(8):
            top = k1 * 32 + block * 8 if block < 4 else 256 + k1 * 8
            value = (mixed_ref[top : top + 8, :128], mixed_ref[top : top + 8, 128:])
            if k1:
                value = cmul(value, (twist_ref[0, k1 : k1 + 1], twist_ref[1, k1 : k1 + 1]))
            values.append(value)
        for n1, value in enumerate(dft(values, 1)):
            lanes = slice(n1 * 128, n1 * 128 + 128)
            rows = slice(block * 8, block * 8 + 8)
            if block < 4:
                value = cmul(value, (lens_ref[0, rows, lanes], lens_ref[1, rows, lanes]))
            else:
                value = cmul(value, (side_lens[0][:, lanes], side_lens[1][:, lanes]))
            for c in range(2):
                if block < 4:
                    lensed_ref[c, 8 + block * 8 : 16 + block * 8, lanes] = value[c]
                else:
                    lensed_ref[c, 7:8, lanes] = value[c][0:1]
                    lensed_ref[c, 40:41, lanes] = value[c][1:2]
    for g in range(8):
        lanes = slice(g * 128, g * 128 + 128)
        beta = (row_ref[0:1, lanes], row_ref[1:2, lanes])
        mid = [lensed_ref[c, 8:40, lanes] for c in range(2)]
        diff = tuple(
            lensed_ref[c, 9:41, lanes] + lensed_ref[c, 7:39, lanes] - 2.0 * mid[c] for c in range(2)
        )
        more = cmul(diff, beta)
        pieces = [split(mid[c] + more[c]) for c in range(2)]
        rhs = [
            jnp.concatenate([pieces[c][part] * own_ref[t, :, :128] for c in range(2) for t in range(4)], axis=0)
            for part in range(2)
        ]
        out = product((mx_ref[0, g], mx_ref[1, g]), rhs)
        across_ref[0, :, lanes] = out[:32]
        across_ref[1, :, lanes] = out[32:]
    lane = lax.broadcasted_iota(jnp.int32, (32, N), 1)
    diff = []
    for c in range(2):
        whole = across_ref[c]
        after = jnp.where(lane == N - 1, 0.0, pltpu.roll(whole, N - 1, 1))
        before = jnp.where(lane == 0, 0.0, pltpu.roll(whole, 1, 1))
        diff.append(after + before - 2.0 * whole)
    more = cmul(diff, (row_ref[0:1], row_ref[1:2]))
    for c in range(2):
        rhs_ref[c] = across_ref[c] + more[c]
    copy.wait()
    for g in range(8):
        lanes = slice(g * 128, g * 128 + 128)
        rhs = jnp.concatenate([rhs_ref[0, :, lanes], rhs_ref[1, :, lanes]], axis=1)
        tiles = [
            jnp.concatenate(
                [mx_ref[part, g, c * 32 : c * 32 + 32] * own_ref[t] for c in range(2) for t in range(4)], axis=0
            )
            for part in range(2)
        ]
        out = product(split(rhs), tiles, NT)
        real_ref[:, lanes] = out[:, :128]
        last = row_ref[4:5, lanes] > 0.5
        for c in range(2):
            out_ref[c, :, lanes] = jnp.where(last, fresh_ref[c, :, lanes], out[:, c * 128 : c * 128 + 128])


def spread_y(field, t):
    half = pltpu.VMEM((256, 256), jnp.bfloat16)
    scratch = [pltpu.VMEM((2, 32, N), jnp.float32), pltpu.VMEM((2, 8, 128), jnp.float32)]
    scratch += [pltpu.VMEM((2, 256, 256), jnp.bfloat16), half, half, pltpu.SemaphoreType.DMA((3,))]
    args = [field, t["twist_y"], t["w1"]]
    return call(forward_y, [shape(32, 8, 256)], scratch, args, large=(0, 1, 2))[0]


def phase_tables(freq, refslow, lat, t):
    args = [freq, refslow, lat, t["x"], t["twist_x"], t["edge"]]
    outs = [shape(2, 256, 128)] + [jax.ShapeDtypeStruct(a.shape, a.dtype) for a in args[3:]]
    return call(phases, outs, [pltpu.SemaphoreType.DMA((3,))], args, scalars=(0, 1, 2), large=(3, 4, 5))


def continue_x(block, tabs):
    scratch = [pltpu.VMEM((256, 256), jnp.bfloat16)] * 2
    return call(along_x, [shape(32, 8, 384)], scratch, [block, *tabs])[0]


def correction_tables(freq, refslow, classes, coupling, last, slow, blocks, t):
    half = jnp.bfloat16
    outs = [shape(2, 32, N), shape(8, N), shape(2, 8, 64, 256, dtype=half)]
    scratch = [pltpu.VMEM((2, 16, 64, 128), half)]
    args = [freq, refslow, classes, coupling, last, slow, blocks, t["own"], t["spread"]]
    return call(weights, outs, scratch, args, scalars=(0, 1, 2, 3, 4))


def correct(block, tabs, up, down, fresh, t):
    plane = pltpu.VMEM((2, 32, N), jnp.float32)
    scratch = [pltpu.VMEM((320, 256), jnp.float32), pltpu.VMEM((2, 48, N), jnp.float32)]
    scratch += [plane, plane, plane, pltpu.SemaphoreType.DMA]
    args = [block, t["w3"], t["twist_y"], *tabs, t["own"], up, down, fresh]
    return call(finish, [shape(2, 32, N), shape(32, N)], scratch, args, large=(9,))


def exchange(block):
    return lax.all_to_all(block, "lat", split_axis=0, concat_axis=0, tiled=True)


def after(value, *others):
    return lax.optimization_barrier((value, others))


def per_device(
    field, fresh, freq_index, ref_slowness, slowness, tile_classes, fd_blocks, fd_coupling, image
):
    t = tables()
    block = spread_y(field.reshape(2, 32, N), t)
    block, (freq, refslow) = after(block, freq_index.reshape(1), ref_slowness)
    received = exchange(block)
    lat = lax.axis_index("lat").reshape(1).astype(jnp.int32)
    block = continue_x(received, phase_tables(freq, refslow, lat, t))
    block, (freq, classes, slow) = after(block, freq, tile_classes.reshape(32), slowness[0])
    received = exchange(block)
    count = lax.axis_size("depth")
    last = (lax.axis_index("depth") == count - 1).reshape(1).astype(jnp.int32)
    tabs = correction_tables(
        freq, refslow, classes, fd_coupling.reshape(32), last, slow, fd_blocks.reshape(1024, 32), t
    )
    tabs, (slow,) = after(tabs, slow)
    down = lax.ppermute(slow[:1], "lat", [(i + 1, i) for i in range(LAT - 1)])
    up = lax.ppermute(slow[-1:], "lat", [(i, i + 1) for i in range(LAT - 1)])
    result, real = correct(received, tabs, up, down, fresh[0], t)
    next_field = lax.ppermute(result, "depth", [(i, (i + 1) % count) for i in range(count)])
    return next_field[None, None], image + real[None]


def solution(mesh):
    return jax.shard_map(
        per_device,
        mesh=mesh,
        in_specs=(
            P("depth", None, None, "lat", None),
            P(None, None, "lat", None),
            P("depth", None),
            P("depth"),
            P("depth", "lat", None),
            P("depth", "lat", None),
            P(),
            P(),
            P("depth", "lat", None),
        ),
        out_specs=(P("depth", None, None, "lat", None), P("depth", "lat", None)),
        check_vma=False,
    )
```

```python
import math

import jax
import jax.numpy as jnp
import ml_dtypes
import numpy as np
from jax import lax
from jax.experimental import pallas as pl
from jax.experimental.pallas import tpu as pltpu
from jax.sharding import PartitionSpec as P

LOW_HZ = 5.0
STEP_HZ = 0.25
DEPTH_KM = 0.01
SPACING_KM = 0.025
N = 1024
LAT = 32
NORM = 1.0 / (N * N)
INTERPRET = False


def parts(values):
    high = values.astype(ml_dtypes.bfloat16)
    low = (values - high.astype(np.float64)).astype(ml_dtypes.bfloat16)
    return np.stack([high, low])


def rotation(angle):
    cos, sin = np.cos(angle), np.sin(angle)
    return np.stack([np.stack([cos, -sin]), np.stack([sin, cos])])


def tables():
    n2 = np.arange(128)
    small = np.arange(32)
    k2 = np.arange(128).reshape(32, 4)
    line = rotation(-2 * np.pi * (k2[:, :, None] * n2 % 128) / 128)
    w1 = line.transpose(2, 0, 3, 1, 4).reshape(256, 256)
    line = rotation(2 * np.pi * (k2[:, :, None] * n2 % 128) / 128)
    w3 = line.transpose(2, 1, 3, 0, 4).reshape(256, 256)
    grid = 2 * np.pi * (small[:, None] * small % 32) / 32
    eye4 = np.eye(4)
    a1 = np.einsum("dcqi,kl->dkqicl", rotation(-grid), eye4).reshape(256, 256)
    a2 = np.einsum("dciq,kl->idkclq", rotation(grid), eye4).reshape(256, 256)
    b1 = np.einsum("dcxp,kl->ckxdlp", rotation(-grid), eye4).reshape(256, 256)
    b2 = np.einsum("dcpx,kl->ckpdlx", rotation(grid), eye4).reshape(256, 256)
    ty = 2 * np.pi * np.arange(8)[:, None] * n2 / N
    tx = np.tile(2 * np.pi * small[:, None] * small / N, (1, 4))
    twist_y = np.stack([np.cos(ty), np.sin(ty)]).astype(np.float32)
    twist_x = np.stack([np.cos(tx), np.sin(tx)]).astype(np.float32)
    edge = np.zeros((8, 32, 8, 8, 2))
    fold = np.zeros((8, 8, 2, 16, 8))
    for k1 in range(8):
        edge[k1, 31, :, k1, 0] = 1
        edge[k1, 0, :, k1, 1] = 1
        for side in range(2):
            fold[:, k1, side, k1, side] = 1
    edge = edge.reshape(256, 128).astype(ml_dtypes.bfloat16)
    fold = fold.reshape(128, 128).astype(ml_dtypes.bfloat16)
    gather = np.repeat(np.eye(32), 8, axis=1).astype(ml_dtypes.bfloat16)
    own = (np.arange(128)[None, :] // 32 == np.arange(4)[:, None]).astype(np.float32)
    own = np.broadcast_to(np.tile(own, (1, 2))[:, None, :], (4, 32, 256)).astype(ml_dtypes.bfloat16)
    spread = np.tile(np.eye(32), (1, 4)).astype(ml_dtypes.bfloat16)
    return {
        "w1": parts(w1),
        "w3": parts(w3),
        "x": np.stack([parts(a1), parts(b1), parts(b2), parts(a2)]),
        "twist_y": twist_y,
        "twist_x": twist_x,
        "edge": edge,
        "fold": fold,
        "gather": gather,
        "own": own,
        "spread": spread,
    }


NN = (((1,), (0,)), ((), ()))
NT = (((1,), (1,)), ((), ()))


def split(values):
    high = values.astype(jnp.bfloat16)
    low = (values - high.astype(jnp.float32)).astype(jnp.bfloat16)
    return high, low


def product(left, right, dims=NN):
    dot = lambda a, b: lax.dot_general(a, b, dims, preferred_element_type=jnp.float32)
    return dot(left[0], right[0]) + (dot(left[1], right[0]) + dot(left[0], right[1]))


def cmul(a, b):
    return a[0] * b[0] - a[1] * b[1], a[0] * b[1] + a[1] * b[0]


def dft(values, sign):
    count = len(values)
    if count == 1:
        return values
    even, odd = dft(values[0::2], sign), dft(values[1::2], sign)
    first, second = [], []
    for k in range(count // 2):
        re, im = odd[k]
        if 4 * k == count:
            re, im = -sign * im, sign * re
        elif k:
            cos = math.cos(2 * math.pi * k / count)
            sin = sign * math.sin(2 * math.pi * k / count)
            if 8 * k == count:
                re, im = cos * (re - sign * im), cos * (im + sign * re)
            else:
                re, im = cmul(odd[k], (cos, sin))
        first.append((even[k][0] + re, even[k][1] + im))
        second.append((even[k][0] - re, even[k][1] - im))
    return first + second


def call(body, outs, scratch, args, scalars=(), large=()):
    size = sum(math.prod(o.shape) * o.dtype.itemsize for o in outs)
    size += sum(math.prod(a.shape) * a.dtype.itemsize for a in args)
    args = [pltpu.with_memory_space_constraint(a, pltpu.HBM) if i in large else a for i, a in enumerate(args)]
    space = lambda i: pltpu.SMEM if i in scalars else pltpu.HBM if i in large else pltpu.VMEM
    return pl.pallas_call(
        body,
        out_shape=outs,
        in_specs=[pl.BlockSpec(memory_space=space(i)) for i in range(len(args))],
        out_specs=[pl.BlockSpec(memory_space=pltpu.VMEM) for _ in outs],
        scratch_shapes=scratch,
        compiler_params=pltpu.CompilerParams(vmem_limit_bytes=24 << 20),
        cost_estimate=pl.CostEstimate(flops=0, bytes_accessed=size, transcendentals=0),
        interpret=INTERPRET,
    )(*args)


def fetch(sources, targets, sems):
    copies = [pltpu.make_async_copy(a, b, sems.at[i]) for i, (a, b) in enumerate(zip(sources, targets, strict=True))]
    for copy in copies:
        copy.start()
    return copies


def shape(*dims, dtype=jnp.float32):
    return jax.ShapeDtypeStruct(dims, dtype)


FIRST = 17
SECOND = 18


def lane_of(dims):
    return lax.broadcasted_iota(jnp.int32, dims, len(dims) - 1)


def forward_y(
    field_any, twist_any, w1_any, slow_any, out_ref,
    field_ref, twist_ref, w1_ref, slow_ref, high_ref, low_ref, ends_ref, sems,
):
    sources = [field_any, twist_any, slow_any.at[0:8], slow_any.at[24:32], w1_any]
    copies = fetch(sources, [field_ref, twist_ref, slow_ref.at[0:8], slow_ref.at[8:16], w1_ref], sems)
    copies[0].wait()
    copies[1].wait()
    for top in range(0, 32, 16):
        rows = slice(top, top + 16)
        lines = [
            tuple(field_ref[c, rows, n1 * 128 : n1 * 128 + 128] for c in range(2)) for n1 in range(8)
        ]
        for k1, value in enumerate(dft(lines, -1)):
            if k1:
                cos, sin = twist_ref[0, k1 : k1 + 1], twist_ref[1, k1 : k1 + 1]
                value = cmul(value, (cos, -sin))
            at = slice(k1 * 32 + top, k1 * 32 + top + 16)
            for c in range(2):
                high, low = split(value[c])
                high_ref[at, c * 128 : c * 128 + 128] = high
                low_ref[at, c * 128 : c * 128 + 128] = low
    copies[2].wait()
    copies[3].wait()
    for n1 in range(8):
        ends_ref[0, n1 : n1 + 1] = slow_ref[0:1, n1 * 128 : n1 * 128 + 128]
        ends_ref[1, n1 : n1 + 1] = slow_ref[15:16, n1 * 128 : n1 * 128 + 128]
    lane = lane_of((8, 128))
    for m in range(4):
        first = pltpu.roll(ends_ref[0], (-32 * m) % 128, 1)
        last = pltpu.roll(ends_ref[1], (32 - 32 * m) % 128, 1)
        out_ref[pl.ds(FIRST * m + 16, 8, stride=4 * FIRST), :] = jnp.where(lane < 32, first, last)
    copies[4].wait()
    out = product((w1_ref[0], w1_ref[1]), (high_ref[...], low_ref[...]), NT)
    for j in range(LAT):
        for half in range(2):
            top = FIRST * j + half * 8
            out_ref[top : top + 8] = out[j * 8 : j * 8 + 8, half * 128 : half * 128 + 128]


def sincos(angle):
    return jnp.cos(angle), jnp.sin(angle)


def phases(
    freq_ref, slow_ref, lat_ref, x_any, twist_any, edge_any, gather_any,
    out_ref, x_ref, twist_ref, edge_ref, gather_ref, sems,
):
    copies = fetch([x_any, twist_any, edge_any, gather_any], [x_ref, twist_ref, edge_ref, gather_ref], sems)
    omega = 2.0 * math.pi * (LOW_HZ + STEP_HZ * freq_ref[0].astype(jnp.float32))
    reach = omega * slow_ref[0]
    scale = 2.0 * math.pi / (N * SPACING_KM)
    for block in range(8):
        h, k2l = block // 4, block % 4
        q = lax.broadcasted_iota(jnp.int32, (32, 128), 0)
        lane = lax.broadcasted_iota(jnp.int32, (32, 128), 1)
        kx = q + 32 * (lane % 32)
        ky = h * 4 + lane // 32 + 8 * (4 * lat_ref[0] + k2l)
        kx = jnp.where(kx < N // 2, kx, kx - N).astype(jnp.float32) * scale
        ky = jnp.where(ky < N // 2, ky, ky - N).astype(jnp.float32) * scale
        square = reach * reach - kx * kx - ky * ky
        root = jnp.sqrt(jnp.abs(square))
        angle = jnp.where(square > 0, root * DEPTH_KM, 0.0)
        amplitude = jnp.where(square > 0, 1.0, jnp.exp(-root * DEPTH_KM))
        cos, sin = sincos(angle)
        out_ref[0, block * 32 : block * 32 + 32] = amplitude * cos
        out_ref[1, block * 32 : block * 32 + 32] = amplitude * sin
    for copy in copies:
        copy.wait()


def both_tiles(ref, rows):
    return [
        jnp.concatenate([ref[rows * i + half * 8 : rows * i + half * 8 + 8] for i in range(LAT)], axis=0) for half in range(2)
    ]


def along_x(in_ref, phase_ref, x_ref, twist_ref, edge_ref, gather_ref, out_ref, high_ref, low_ref):
    lines = jnp.concatenate(both_tiles(in_ref, FIRST), axis=1)
    mixed = product((x_ref[0, 0], x_ref[0, 1]), split(lines))
    cos, sin = twist_ref[0], twist_ref[1]

    def put(at, value):
        for c in range(2):
            high, low = split(value[c])
            high_ref[at, c * 128 : c * 128 + 128] = high
            low_ref[at, c * 128 : c * 128 + 128] = low

    for h in range(2):
        lanes = slice(h * 128, h * 128 + 128)
        for k2l in range(4):
            value = (mixed[k2l * 32 : k2l * 32 + 32, lanes], mixed[128 + k2l * 32 : 160 + k2l * 32, lanes])
            top = (h * 4 + k2l) * 32
            put(slice(top, top + 32), cmul(value, (cos, -sin)))
    spectrum = product((high_ref[...], low_ref[...]), (x_ref[1, 0], x_ref[1, 1]))
    for block in range(8):
        rows = slice(block * 32, block * 32 + 32)
        value = (spectrum[rows, :128], spectrum[rows, 128:])
        put(rows, cmul(value, (phase_ref[0, rows], phase_ref[1, rows])))
    mixed = product((high_ref[...], low_ref[...]), (x_ref[2, 0], x_ref[2, 1]))
    for h in range(2):
        for k2l in range(4):
            rows = slice((h * 4 + k2l) * 32, (h * 4 + k2l) * 32 + 32)
            value = cmul((mixed[rows, :128], mixed[rows, 128:]), (cos, sin))
            for c in range(2):
                high, low = split(value[c])
                at = slice(c * 128 + k2l * 32, c * 128 + k2l * 32 + 32)
                high_ref[at, h * 128 : h * 128 + 128] = high
                low_ref[at, h * 128 : h * 128 + 128] = low
    out = product((x_ref[3, 0], x_ref[3, 1]), (high_ref[...], low_ref[...]))
    for i in range(LAT):
        for half in range(2):
            top = SECOND * i + half * 8
            out_ref[top : top + 8] = out[i * 8 : i * 8 + 8, half * 128 : half * 128 + 128]
    dot = lambda a, b: lax.dot_general(a, b, NN, preferred_element_type=jnp.float32)
    high, low = split(out)
    edge = dot(high, edge_ref[...]) + dot(low, edge_ref[...])
    own = lane_of((256, 128)) // 16 == lax.broadcasted_iota(jnp.int32, (256, 128), 0) % 8
    high, low = split(jnp.where(own, edge, 0.0))
    edge = dot(gather_ref[...], high) + dot(gather_ref[...], low)
    lane, row = lane_of((LAT, 128)), lax.broadcasted_iota(jnp.int32, (LAT, 128), 0)
    before = jnp.where(row == 0, 0.0, pltpu.roll(edge, 1, 0))
    after = jnp.where(row == LAT - 1, 0.0, pltpu.roll(edge, LAT - 1, 0))
    out_ref[pl.ds(16, LAT, stride=SECOND), :] = jnp.where(lane % 2 == 0, before, after)
    slow = in_ref[pl.ds(16, LAT, stride=FIRST), :]
    before = pltpu.roll(pltpu.roll(slow, 96, 1), 1, 0)
    after = pltpu.roll(pltpu.roll(slow, 32, 1), LAT - 1, 0)
    out_ref[pl.ds(17, LAT, stride=SECOND), :] = jnp.where(lane < 32, before, after)


def weights(
    freq_ref, refslow_ref, class_ref, coupling_ref, last_ref, slow_ref, blocks_ref, own_ref, spread_ref,
    lens_ref, row_ref, mx_ref, wide_ref,
):
    omega = 2.0 * math.pi * (LOW_HZ + STEP_HZ * freq_ref[0].astype(jnp.float32))
    base = refslow_ref[0]
    for top in range(0, 32, 8):
        rows = slice(top, top + 8)
        cos, sin = sincos(omega * (slow_ref[rows] - base) * DEPTH_KM)
        lens_ref[0, rows], lens_ref[1, rows] = cos * NORM, sin * NORM
    high, low = split(blocks_ref[...])
    dot = lambda a: lax.dot_general(a, spread_ref[...], NN, preferred_element_type=jnp.float32)
    wide_ref[0] = dot(high).astype(jnp.bfloat16).reshape(16, 64, 128)
    wide_ref[1] = dot(low).astype(jnp.bfloat16).reshape(16, 64, 128)
    row_ref[2:3] = jnp.full((1, N), omega)
    row_ref[3:4] = jnp.full((1, N), base)
    row_ref[4:5] = jnp.full((1, N), last_ref[0].astype(jnp.float32))
    lane = lax.broadcasted_iota(jnp.int32, (1, 128), 1) // 32
    for g in range(8):
        classes = [class_ref[g * 4 + t] for t in range(4)]
        for c in range(2):
            beta = jnp.full((1, 128), coupling_ref[classes[0] * 2 + c])
            for t in range(1, 4):
                beta = jnp.where(lane == t, coupling_ref[classes[t] * 2 + c], beta)
            row_ref[c : c + 1, g * 128 : g * 128 + 128] = beta
        for part in range(2):
            total = []
            for c in range(2):
                tiles = [wide_ref[part, classes[t], c * 32 : c * 32 + 32] * own_ref[t, :, :128] for t in range(4)]
                total.append((tiles[0] + tiles[1]) + (tiles[2] + tiles[3]))
            mx_ref[part, g, :32, :128] = total[0]
            mx_ref[part, g, :32, 128:] = -total[1]
            mx_ref[part, g, 32:, :128] = total[1]
            mx_ref[part, g, 32:, 128:] = total[0]


def finish(
    in_ref, w3_ref, twist_ref, lens_ref, row_ref, mx_ref, own_ref, fold_ref, fresh_any,
    out_ref, real_ref, mixed_ref, lensed_ref, rhs_ref, across_ref, fresh_ref, sem,
):
    copy = pltpu.make_async_copy(fresh_any, fresh_ref, sem)
    copy.start()
    lane = lane_of((8, 128))
    sides = [None, None]
    for m in range(4):
        pieces = in_ref[pl.ds(17 + SECOND * m, 8, stride=4 * SECOND), :]
        for side in range(2):
            piece = pltpu.roll(pieces, (32 * m - 32 * side) % 128, 1)
            sides[side] = piece if m == 0 else jnp.where(lane // 32 == m, piece, sides[side])
    side_lens = []
    for side in range(2):
        cos, sin = sincos(row_ref[2:3, :128] * (sides[side] - row_ref[3:4, :128]) * DEPTH_KM)
        side_lens.append((cos * NORM, sin * NORM))
    beside = jnp.concatenate(
        [jnp.broadcast_to(in_ref[SECOND * j + 16 : SECOND * j + 17], (8, 128)) for j in range(LAT)], axis=0
    )
    own = lane_of((256, 128)) // 16 == lax.broadcasted_iota(jnp.int32, (256, 128), 0) % 8
    high, low = split(jnp.where(own, beside, 0.0))
    dot = lambda a: lax.dot_general(a, fold_ref[...], NN, preferred_element_type=jnp.float32)
    lines = [*both_tiles(in_ref, SECOND), dot(high) + dot(low)]
    turned = jnp.concatenate([line.T for line in lines], axis=0)[:320]
    mixed_ref[...] = product(split(turned), (w3_ref[0], w3_ref[1]))
    for block in range(5):
        values = []
        for k1 in range(8):
            top = k1 * 32 + block * 8 if block < 4 else 256 + k1 * 8
            value = (mixed_ref[top : top + 8, :128], mixed_ref[top : top + 8, 128:])
            if k1:
                value = cmul(value, (twist_ref[0, k1 : k1 + 1], twist_ref[1, k1 : k1 + 1]))
            values.append(value)
        for n1, value in enumerate(dft(values, 1)):
            lanes = slice(n1 * 128, n1 * 128 + 128)
            rows = slice(block * 8, block * 8 + 8)
            if block < 4:
                value = cmul(value, (lens_ref[0, rows, lanes], lens_ref[1, rows, lanes]))
                for c in range(2):
                    lensed_ref[c, 8 + block * 8 : 16 + block * 8, lanes] = value[c]
                continue
            for side, at in enumerate((7, 40)):
                pair = [value[c][side : side + 1] for c in range(2)]
                pair = cmul(pair, [side_lens[side][c][n1 : n1 + 1] for c in range(2)])
                for c in range(2):
                    lensed_ref[c, at : at + 1, lanes] = pair[c]
    for g in range(8):
        lanes = slice(g * 128, g * 128 + 128)
        beta = (row_ref[0:1, lanes], row_ref[1:2, lanes])
        mid = [lensed_ref[c, 8:40, lanes] for c in range(2)]
        diff = tuple(
            lensed_ref[c, 9:41, lanes] + lensed_ref[c, 7:39, lanes] - 2.0 * mid[c] for c in range(2)
        )
        more = cmul(diff, beta)
        pieces = [split(mid[c] + more[c]) for c in range(2)]
        rhs = [
            jnp.concatenate([pieces[c][part] * own_ref[t, :, :128] for c in range(2) for t in range(4)], axis=0)
            for part in range(2)
        ]
        out = product((mx_ref[0, g], mx_ref[1, g]), rhs)
        across_ref[0, :, lanes] = out[:32]
        across_ref[1, :, lanes] = out[32:]
    lane = lax.broadcasted_iota(jnp.int32, (32, N), 1)
    diff = []
    for c in range(2):
        whole = across_ref[c]
        after = jnp.where(lane == N - 1, 0.0, pltpu.roll(whole, N - 1, 1))
        before = jnp.where(lane == 0, 0.0, pltpu.roll(whole, 1, 1))
        diff.append(after + before - 2.0 * whole)
    more = cmul(diff, (row_ref[0:1], row_ref[1:2]))
    for c in range(2):
        rhs_ref[c] = across_ref[c] + more[c]
    copy.wait()
    for g in range(8):
        lanes = slice(g * 128, g * 128 + 128)
        rhs = jnp.concatenate([rhs_ref[0, :, lanes], rhs_ref[1, :, lanes]], axis=1)
        tiles = [
            jnp.concatenate(
                [mx_ref[part, g, c * 32 : c * 32 + 32] * own_ref[t] for c in range(2) for t in range(4)], axis=0
            )
            for part in range(2)
        ]
        out = product(split(rhs), tiles, NT)
        real_ref[:, lanes] = out[:, :128]
        last = row_ref[4:5, lanes] > 0.5
        for c in range(2):
            out_ref[c, :, lanes] = jnp.where(last, fresh_ref[c, :, lanes], out[:, c * 128 : c * 128 + 128])


def spread_y(field, slow, t):
    half = pltpu.VMEM((256, 256), jnp.bfloat16)
    scratch = [pltpu.VMEM((2, 32, N), jnp.float32), pltpu.VMEM((2, 8, 128), jnp.float32)]
    scratch += [pltpu.VMEM((2, 256, 256), jnp.bfloat16), pltpu.VMEM((16, N), jnp.float32), half, half]
    scratch += [pltpu.VMEM((2, 8, 128), jnp.float32), pltpu.SemaphoreType.DMA((5,))]
    args = [field, t["twist_y"], t["w1"], slow]
    return call(forward_y, [shape(LAT * FIRST, 128)], scratch, args, large=(0, 1, 2, 3))[0]


def phase_tables(freq, refslow, lat, t):
    args = [freq, refslow, lat, t["x"], t["twist_x"], t["edge"], t["gather"]]
    outs = [shape(2, 256, 128)] + [jax.ShapeDtypeStruct(a.shape, a.dtype) for a in args[3:]]
    return call(phases, outs, [pltpu.SemaphoreType.DMA((4,))], args, scalars=(0, 1, 2), large=(3, 4, 5, 6))


def continue_x(block, tabs):
    scratch = [pltpu.VMEM((256, 256), jnp.bfloat16)] * 2
    return call(along_x, [shape(LAT * SECOND, 128)], scratch, [block, *tabs])[0]


def correction_tables(freq, refslow, classes, coupling, last, slow, blocks, t):
    half = jnp.bfloat16
    outs = [shape(2, 32, N), shape(8, N), shape(2, 8, 64, 256, dtype=half)]
    scratch = [pltpu.VMEM((2, 16, 64, 128), half)]
    args = [freq, refslow, classes, coupling, last, slow, blocks, t["own"], t["spread"]]
    return call(weights, outs, scratch, args, scalars=(0, 1, 2, 3, 4))


def correct(block, tabs, fresh, t):
    plane = pltpu.VMEM((2, 32, N), jnp.float32)
    scratch = [pltpu.VMEM((320, 256), jnp.float32), pltpu.VMEM((2, 48, N), jnp.float32)]
    scratch += [plane, plane, plane, pltpu.SemaphoreType.DMA]
    args = [block, t["w3"], t["twist_y"], *tabs, t["own"], t["fold"], fresh]
    return call(finish, [shape(2, 32, N), shape(32, N)], scratch, args, large=(8,))


def exchange(block):
    blocks = block.reshape(LAT, 1, -1)
    return lax.all_to_all(blocks, "lat", split_axis=0, concat_axis=0, tiled=True).reshape(block.shape)


def after(value, *others):
    return lax.optimization_barrier((value, others))


def per_device(
    field, fresh, freq_index, ref_slowness, slowness, tile_classes, fd_blocks, fd_coupling, image
):
    t = tables()
    slow = slowness[0]
    block = spread_y(field.reshape(2, 32, N), slow, t)
    block, (freq, refslow) = after(block, freq_index.reshape(1), ref_slowness)
    received = exchange(block)
    lat = lax.axis_index("lat").reshape(1).astype(jnp.int32)
    block = continue_x(received, phase_tables(freq, refslow, lat, t))
    block, (freq, classes, slow) = after(block, freq, tile_classes.reshape(32), slow)
    received = exchange(block)
    count = lax.axis_size("depth")
    last = (lax.axis_index("depth") == count - 1).reshape(1).astype(jnp.int32)
    tabs = correction_tables(
        freq, refslow, classes, fd_coupling.reshape(32), last, slow, fd_blocks.reshape(1024, 32), t
    )
    result, real = correct(received, tabs, fresh[0], t)
    next_field = lax.ppermute(result, "depth", [(i, (i + 1) % count) for i in range(count)])
    return next_field[None, None], image + real[None]


def solution(mesh):
    return jax.shard_map(
        per_device,
        mesh=mesh,
        in_specs=(
            P("depth", None, None, "lat", None),
            P(None, None, "lat", None),
            P("depth", None),
            P("depth"),
            P("depth", "lat", None),
            P("depth", "lat", None),
            P(),
            P(),
            P("depth", "lat", None),
        ),
        out_specs=(P("depth", None, None, "lat", None), P("depth", "lat", None)),
        check_vma=False,
    )
```

```python
import math

import jax
import jax.numpy as jnp
import ml_dtypes
import numpy as np
from jax import lax
from jax.experimental import pallas as pl
from jax.experimental.pallas import tpu as pltpu
from jax.sharding import PartitionSpec as P

LOW_HZ = 5.0
STEP_HZ = 0.25
DEPTH_KM = 0.01
SPACING_KM = 0.025
N = 1024
LAT = 32
NORM = 1.0 / (N * N)
INTERPRET = False


def parts(values):
    high = values.astype(ml_dtypes.bfloat16)
    low = (values - high.astype(np.float64)).astype(ml_dtypes.bfloat16)
    return np.stack([high, low])


def rotation(angle):
    cos, sin = np.cos(angle), np.sin(angle)
    return np.stack([np.stack([cos, -sin]), np.stack([sin, cos])])


def tables():
    n2 = np.arange(128)
    small = np.arange(32)
    k2 = np.arange(128).reshape(32, 4)
    line = rotation(-2 * np.pi * (k2[:, :, None] * n2 % 128) / 128)
    w1 = line.transpose(2, 0, 3, 1, 4).reshape(256, 256)
    line = rotation(2 * np.pi * (k2[:, :, None] * n2 % 128) / 128)
    w3 = line.transpose(2, 1, 3, 0, 4).reshape(256, 256)
    grid = 2 * np.pi * (small[:, None] * small % 32) / 32
    eye4 = np.eye(4)
    a1 = np.einsum("dcqi,kl->dkqicl", rotation(-grid), eye4).reshape(256, 256)
    a2 = np.einsum("dciq,kl->idkclq", rotation(grid), eye4).reshape(256, 256)
    b1 = np.einsum("dcxp,kl->ckxdlp", rotation(-grid), eye4).reshape(256, 256)
    b2 = np.einsum("dcpx,kl->ckpdlx", rotation(grid), eye4).reshape(256, 256)
    ty = 2 * np.pi * np.arange(8)[:, None] * n2 / N
    tx = np.tile(2 * np.pi * small[:, None] * small / N, (1, 4))
    twist_y = np.stack([np.cos(ty), np.sin(ty)]).astype(np.float32)
    twist_x = np.stack([np.cos(tx), np.sin(tx)]).astype(np.float32)
    edge = np.zeros((8, 32, 8, 8, 2))
    fold = np.zeros((8, 8, 2, 16, 8))
    for k1 in range(8):
        edge[k1, 31, :, k1, 0] = 1
        edge[k1, 0, :, k1, 1] = 1
        for side in range(2):
            fold[:, k1, side, k1, side] = 1
    edge = edge.reshape(256, 128).astype(ml_dtypes.bfloat16)
    fold = fold.reshape(128, 128).astype(ml_dtypes.bfloat16)
    gather = np.repeat(np.eye(32), 8, axis=1).astype(ml_dtypes.bfloat16)
    own = (np.arange(128)[None, :] // 32 == np.arange(4)[:, None]).astype(np.float32)
    own = np.broadcast_to(np.tile(own, (1, 2))[:, None, :], (4, 32, 256)).astype(ml_dtypes.bfloat16)
    spread = np.tile(np.eye(32), (1, 4)).astype(ml_dtypes.bfloat16)
    return {
        "w1": parts(w1),
        "w3": parts(w3),
        "x": np.stack([parts(a1), parts(b1), parts(b2), parts(a2)]),
        "twist_y": twist_y,
        "twist_x": twist_x,
        "edge": edge,
        "fold": fold,
        "gather": gather,
        "own": own,
        "spread": spread,
    }


NN = (((1,), (0,)), ((), ()))
NT = (((1,), (1,)), ((), ()))


def split(values):
    high = values.astype(jnp.bfloat16)
    low = (values - high.astype(jnp.float32)).astype(jnp.bfloat16)
    return high, low


def product(left, right, dims=NN):
    dot = lambda a, b: lax.dot_general(a, b, dims, preferred_element_type=jnp.float32)
    rows = left[0].shape[0]
    both = dot(jnp.concatenate(left, axis=0), right[0])
    return both[:rows] + (both[rows:] + dot(left[0], right[1]))


def cmul(a, b):
    return a[0] * b[0] - a[1] * b[1], a[0] * b[1] + a[1] * b[0]


def dft(values, sign):
    count = len(values)
    if count == 1:
        return values
    even, odd = dft(values[0::2], sign), dft(values[1::2], sign)
    first, second = [], []
    for k in range(count // 2):
        re, im = odd[k]
        if 4 * k == count:
            re, im = -sign * im, sign * re
        elif k:
            cos = math.cos(2 * math.pi * k / count)
            sin = sign * math.sin(2 * math.pi * k / count)
            if 8 * k == count:
                re, im = cos * (re - sign * im), cos * (im + sign * re)
            else:
                re, im = cmul(odd[k], (cos, sin))
        first.append((even[k][0] + re, even[k][1] + im))
        second.append((even[k][0] - re, even[k][1] - im))
    return first + second


def call(body, outs, scratch, args, scalars=(), large=()):
    size = sum(math.prod(o.shape) * o.dtype.itemsize for o in outs)
    size += sum(math.prod(a.shape) * a.dtype.itemsize for a in args)
    args = [pltpu.with_memory_space_constraint(a, pltpu.HBM) if i in large else a for i, a in enumerate(args)]
    space = lambda i: pltpu.SMEM if i in scalars else pltpu.HBM if i in large else pltpu.VMEM
    return pl.pallas_call(
        body,
        out_shape=outs,
        in_specs=[pl.BlockSpec(memory_space=space(i)) for i in range(len(args))],
        out_specs=[pl.BlockSpec(memory_space=pltpu.VMEM) for _ in outs],
        scratch_shapes=scratch,
        compiler_params=pltpu.CompilerParams(vmem_limit_bytes=24 << 20),
        cost_estimate=pl.CostEstimate(flops=0, bytes_accessed=size, transcendentals=0),
        interpret=INTERPRET,
    )(*args)


def fetch(sources, targets, sems):
    copies = [pltpu.make_async_copy(a, b, sems.at[i]) for i, (a, b) in enumerate(zip(sources, targets, strict=True))]
    for copy in copies:
        copy.start()
    return copies


def shape(*dims, dtype=jnp.float32):
    return jax.ShapeDtypeStruct(dims, dtype)


FIRST = 17
SECOND = 18


def lane_of(dims):
    return lax.broadcasted_iota(jnp.int32, dims, len(dims) - 1)


def forward_y(
    field_any, twist_any, w1_any, slow_any, out_ref,
    field_ref, twist_ref, w1_ref, slow_ref, high_ref, low_ref, ends_ref, sems,
):
    sources = [field_any, twist_any, slow_any.at[0:8], slow_any.at[24:32], w1_any]
    copies = fetch(sources, [field_ref, twist_ref, slow_ref.at[0:8], slow_ref.at[8:16], w1_ref], sems)
    copies[0].wait()
    copies[1].wait()
    for top in range(0, 32, 16):
        rows = slice(top, top + 16)
        lines = [
            tuple(field_ref[c, rows, n1 * 128 : n1 * 128 + 128] for c in range(2)) for n1 in range(8)
        ]
        for k1, value in enumerate(dft(lines, -1)):
            if k1:
                cos, sin = twist_ref[0, k1 : k1 + 1], twist_ref[1, k1 : k1 + 1]
                value = cmul(value, (cos, -sin))
            at = slice(k1 * 32 + top, k1 * 32 + top + 16)
            for c in range(2):
                high, low = split(value[c])
                high_ref[at, c * 128 : c * 128 + 128] = high
                low_ref[at, c * 128 : c * 128 + 128] = low
    copies[2].wait()
    copies[3].wait()
    for n1 in range(8):
        ends_ref[0, n1 : n1 + 1] = slow_ref[0:1, n1 * 128 : n1 * 128 + 128]
        ends_ref[1, n1 : n1 + 1] = slow_ref[15:16, n1 * 128 : n1 * 128 + 128]
    lane = lane_of((8, 128))
    for m in range(4):
        first = pltpu.roll(ends_ref[0], (-32 * m) % 128, 1)
        last = pltpu.roll(ends_ref[1], (32 - 32 * m) % 128, 1)
        out_ref[pl.ds(FIRST * m + 16, 8, stride=4 * FIRST), :] = jnp.where(lane < 32, first, last)
    copies[4].wait()
    out = product((w1_ref[0], w1_ref[1]), (high_ref[...], low_ref[...]), NT)
    for j in range(LAT):
        for half in range(2):
            top = FIRST * j + half * 8
            out_ref[top : top + 8] = out[j * 8 : j * 8 + 8, half * 128 : half * 128 + 128]


def sincos(angle):
    return jnp.cos(angle), jnp.sin(angle)


def phases(
    freq_ref, slow_ref, lat_ref, x_any, twist_any, edge_any, gather_any,
    out_ref, x_ref, twist_ref, edge_ref, gather_ref, sems,
):
    copies = fetch([x_any, twist_any, edge_any, gather_any], [x_ref, twist_ref, edge_ref, gather_ref], sems)
    omega = 2.0 * math.pi * (LOW_HZ + STEP_HZ * freq_ref[0].astype(jnp.float32))
    reach = omega * slow_ref[0]
    scale = 2.0 * math.pi / (N * SPACING_KM)
    for block in range(8):
        h, k2l = block // 4, block % 4
        q = lax.broadcasted_iota(jnp.int32, (32, 128), 0)
        lane = lax.broadcasted_iota(jnp.int32, (32, 128), 1)
        kx = q + 32 * (lane % 32)
        ky = h * 4 + lane // 32 + 8 * (4 * lat_ref[0] + k2l)
        kx = jnp.where(kx < N // 2, kx, kx - N).astype(jnp.float32) * scale
        ky = jnp.where(ky < N // 2, ky, ky - N).astype(jnp.float32) * scale
        square = reach * reach - kx * kx - ky * ky
        root = jnp.sqrt(jnp.abs(square))
        angle = jnp.where(square > 0, root * DEPTH_KM, 0.0)
        amplitude = jnp.where(square > 0, 1.0, jnp.exp(-root * DEPTH_KM))
        cos, sin = sincos(angle)
        out_ref[0, block * 32 : block * 32 + 32] = amplitude * cos
        out_ref[1, block * 32 : block * 32 + 32] = amplitude * sin
    for copy in copies:
        copy.wait()


def both_tiles(ref, rows):
    return [
        jnp.concatenate([ref[rows * i + half * 8 : rows * i + half * 8 + 8] for i in range(LAT)], axis=0) for half in range(2)
    ]


def along_x(in_ref, phase_ref, x_ref, twist_ref, edge_ref, gather_ref, out_ref, high_ref, low_ref):
    lines = jnp.concatenate(both_tiles(in_ref, FIRST), axis=1)
    mixed = product((x_ref[0, 0], x_ref[0, 1]), split(lines))
    cos, sin = twist_ref[0], twist_ref[1]

    def put(at, value):
        for c in range(2):
            high, low = split(value[c])
            high_ref[at, c * 128 : c * 128 + 128] = high
            low_ref[at, c * 128 : c * 128 + 128] = low

    for h in range(2):
        lanes = slice(h * 128, h * 128 + 128)
        for k2l in range(4):
            value = (mixed[k2l * 32 : k2l * 32 + 32, lanes], mixed[128 + k2l * 32 : 160 + k2l * 32, lanes])
            top = (h * 4 + k2l) * 32
            put(slice(top, top + 32), cmul(value, (cos, -sin)))
    spectrum = product((high_ref[...], low_ref[...]), (x_ref[1, 0], x_ref[1, 1]))
    for block in range(8):
        rows = slice(block * 32, block * 32 + 32)
        value = (spectrum[rows, :128], spectrum[rows, 128:])
        put(rows, cmul(value, (phase_ref[0, rows], phase_ref[1, rows])))
    mixed = product((high_ref[...], low_ref[...]), (x_ref[2, 0], x_ref[2, 1]))
    for h in range(2):
        for k2l in range(4):
            rows = slice((h * 4 + k2l) * 32, (h * 4 + k2l) * 32 + 32)
            value = cmul((mixed[rows, :128], mixed[rows, 128:]), (cos, sin))
            for c in range(2):
                high, low = split(value[c])
                at = slice(c * 128 + k2l * 32, c * 128 + k2l * 32 + 32)
                high_ref[at, h * 128 : h * 128 + 128] = high
                low_ref[at, h * 128 : h * 128 + 128] = low
    out = product((x_ref[3, 0], x_ref[3, 1]), (high_ref[...], low_ref[...]))
    for i in range(LAT):
        for half in range(2):
            top = SECOND * i + half * 8
            out_ref[top : top + 8] = out[i * 8 : i * 8 + 8, half * 128 : half * 128 + 128]
    dot = lambda a, b: lax.dot_general(a, b, NN, preferred_element_type=jnp.float32)
    high, low = split(out)
    edge = dot(high, edge_ref[...]) + dot(low, edge_ref[...])
    own = lane_of((256, 128)) // 16 == lax.broadcasted_iota(jnp.int32, (256, 128), 0) % 8
    high, low = split(jnp.where(own, edge, 0.0))
    edge = dot(gather_ref[...], high) + dot(gather_ref[...], low)
    lane, row = lane_of((LAT, 128)), lax.broadcasted_iota(jnp.int32, (LAT, 128), 0)
    before = jnp.where(row == 0, 0.0, pltpu.roll(edge, 1, 0))
    after = jnp.where(row == LAT - 1, 0.0, pltpu.roll(edge, LAT - 1, 0))
    out_ref[pl.ds(16, LAT, stride=SECOND), :] = jnp.where(lane % 2 == 0, before, after)
    slow = in_ref[pl.ds(16, LAT, stride=FIRST), :]
    before = pltpu.roll(pltpu.roll(slow, 96, 1), 1, 0)
    after = pltpu.roll(pltpu.roll(slow, 32, 1), LAT - 1, 0)
    out_ref[pl.ds(17, LAT, stride=SECOND), :] = jnp.where(lane < 32, before, after)


def weights(
    freq_ref, refslow_ref, class_ref, coupling_ref, last_ref, slow_ref, blocks_ref, own_ref, spread_ref,
    lens_ref, row_ref, mx_ref, my_ref, wide_ref,
):
    omega = 2.0 * math.pi * (LOW_HZ + STEP_HZ * freq_ref[0].astype(jnp.float32))
    base = refslow_ref[0]
    for top in range(0, 32, 8):
        rows = slice(top, top + 8)
        cos, sin = sincos(omega * (slow_ref[rows] - base) * DEPTH_KM)
        lens_ref[0, rows], lens_ref[1, rows] = cos * NORM, sin * NORM
    high, low = split(blocks_ref[...])
    dot = lambda a: lax.dot_general(a, spread_ref[...], NN, preferred_element_type=jnp.float32)
    wide_ref[0] = dot(high).astype(jnp.bfloat16).reshape(2, 16, 64, 128)
    wide_ref[1] = dot(low).astype(jnp.bfloat16).reshape(2, 16, 64, 128)
    row_ref[2:3] = jnp.full((1, N), omega)
    row_ref[3:4] = jnp.full((1, N), base)
    row_ref[4:5] = jnp.full((1, N), last_ref[0].astype(jnp.float32))
    lane = lax.broadcasted_iota(jnp.int32, (1, 128), 1) // 32
    for g in range(8):
        classes = [class_ref[g * 4 + t] for t in range(4)]
        for c in range(2):
            beta = jnp.full((1, 128), coupling_ref[classes[0] * 2 + c])
            for t in range(1, 4):
                beta = jnp.where(lane == t, coupling_ref[classes[t] * 2 + c], beta)
            row_ref[c : c + 1, g * 128 : g * 128 + 128] = beta
        for part in range(2):
            total = []
            for turned in range(2):
                for c in range(2):
                    own = [
                        wide_ref[part, turned, classes[t], c * 32 : c * 32 + 32] * own_ref[t, :, :128] for t in range(4)
                    ]
                    total.append((own[0] + own[1]) + (own[2] + own[3]))
            mx_ref[part, g, :32, :128] = total[0]
            mx_ref[part, g, :32, 128:] = -total[1]
            mx_ref[part, g, 32:, :128] = total[1]
            mx_ref[part, g, 32:, 128:] = total[0]
            my_ref[part, g, :32, :128] = total[2]
            my_ref[part, g, :32, 128:] = total[3]
            my_ref[part, g, 32:, :128] = -total[3]
            my_ref[part, g, 32:, 128:] = total[2]


def finish(
    in_ref, w3_ref, twist_ref, lens_ref, row_ref, mx_ref, my_ref, own_ref, fold_ref, fresh_any,
    out_ref, real_ref, mixed_ref, lensed_ref, rhs_ref, across_ref, fresh_ref, sem,
):
    copy = pltpu.make_async_copy(fresh_any, fresh_ref, sem)
    copy.start()
    lane = lane_of((8, 128))
    sides = [None, None]
    for m in range(4):
        pieces = in_ref[pl.ds(17 + SECOND * m, 8, stride=4 * SECOND), :]
        for side in range(2):
            piece = pltpu.roll(pieces, (32 * m - 32 * side) % 128, 1)
            sides[side] = piece if m == 0 else jnp.where(lane // 32 == m, piece, sides[side])
    side_lens = []
    for side in range(2):
        cos, sin = sincos(row_ref[2:3, :128] * (sides[side] - row_ref[3:4, :128]) * DEPTH_KM)
        side_lens.append((cos * NORM, sin * NORM))
    beside = jnp.concatenate(
        [jnp.broadcast_to(in_ref[SECOND * j + 16 : SECOND * j + 17], (8, 128)) for j in range(LAT)], axis=0
    )
    own = lane_of((256, 128)) // 16 == lax.broadcasted_iota(jnp.int32, (256, 128), 0) % 8
    high, low = split(jnp.where(own, beside, 0.0))
    dot = lambda a: lax.dot_general(a, fold_ref[...], NN, preferred_element_type=jnp.float32)
    lines = [*both_tiles(in_ref, SECOND), dot(high) + dot(low)]
    turned = jnp.concatenate([line.T for line in lines], axis=0)[:320]
    mixed_ref[...] = product(split(turned), (w3_ref[0], w3_ref[1]))
    for block in range(5):
        values = []
        for k1 in range(8):
            top = k1 * 32 + block * 8 if block < 4 else 256 + k1 * 8
            value = (mixed_ref[top : top + 8, :128], mixed_ref[top : top + 8, 128:])
            if k1:
                value = cmul(value, (twist_ref[0, k1 : k1 + 1], twist_ref[1, k1 : k1 + 1]))
            values.append(value)
        for n1, value in enumerate(dft(values, 1)):
            lanes = slice(n1 * 128, n1 * 128 + 128)
            rows = slice(block * 8, block * 8 + 8)
            if block < 4:
                value = cmul(value, (lens_ref[0, rows, lanes], lens_ref[1, rows, lanes]))
                for c in range(2):
                    lensed_ref[c, 8 + block * 8 : 16 + block * 8, lanes] = value[c]
                continue
            for side, at in enumerate((7, 40)):
                pair = [value[c][side : side + 1] for c in range(2)]
                pair = cmul(pair, [side_lens[side][c][n1 : n1 + 1] for c in range(2)])
                for c in range(2):
                    lensed_ref[c, at : at + 1, lanes] = pair[c]
    for g in range(0, 8, 2):
        pair = []
        for lanes in (slice(g * 128, g * 128 + 128), slice(g * 128 + 128, g * 128 + 256)):
            beta = (row_ref[0:1, lanes], row_ref[1:2, lanes])
            mid = [lensed_ref[c, 8:40, lanes] for c in range(2)]
            diff = tuple(
                lensed_ref[c, 9:41, lanes] + lensed_ref[c, 7:39, lanes] - 2.0 * mid[c] for c in range(2)
            )
            more = cmul(diff, beta)
            pair.append([split(mid[c] + more[c]) for c in range(2)])
        rhs = [
            jnp.concatenate(
                [
                    jnp.concatenate([pieces[c][part] * own_ref[t, :, :128] for pieces in pair], axis=1)
                    for c in range(2)
                    for t in range(4)
                ],
                axis=0,
            )
            for part in range(2)
        ]
        left = [jnp.concatenate([mx_ref[part, g], mx_ref[part, g + 1]], axis=0) for part in range(2)]
        out = product(left, rhs)
        for c in range(2):
            across_ref[c, :, g * 128 : g * 128 + 128] = out[c * 32 : c * 32 + 32, :128]
            across_ref[c, :, g * 128 + 128 : g * 128 + 256] = out[64 + c * 32 : 96 + c * 32, 128:]
    lane = lax.broadcasted_iota(jnp.int32, (32, N), 1)
    diff = []
    for c in range(2):
        whole = across_ref[c]
        after = jnp.where(lane == N - 1, 0.0, pltpu.roll(whole, N - 1, 1))
        before = jnp.where(lane == 0, 0.0, pltpu.roll(whole, 1, 1))
        diff.append(after + before - 2.0 * whole)
    more = cmul(diff, (row_ref[0:1], row_ref[1:2]))
    for c in range(2):
        rhs_ref[c] = across_ref[c] + more[c]
    copy.wait()
    for g in range(8):
        lanes = slice(g * 128, g * 128 + 128)
        rhs = jnp.concatenate([rhs_ref[0, :, lanes], rhs_ref[1, :, lanes]], axis=1)
        tiles = [
            jnp.concatenate(
                [my_ref[part, g, c * 32 : c * 32 + 32] * own_ref[t] for c in range(2) for t in range(4)], axis=0
            )
            for part in range(2)
        ]
        out = product(split(rhs), tiles, NN)
        real_ref[:, lanes] = out[:, :128]
        last = row_ref[4:5, lanes] > 0.5
        for c in range(2):
            out_ref[c, :, lanes] = jnp.where(last, fresh_ref[c, :, lanes], out[:, c * 128 : c * 128 + 128])


def spread_y(field, slow, t):
    half = pltpu.VMEM((256, 256), jnp.bfloat16)
    scratch = [pltpu.VMEM((2, 32, N), jnp.float32), pltpu.VMEM((2, 8, 128), jnp.float32)]
    scratch += [pltpu.VMEM((2, 256, 256), jnp.bfloat16), pltpu.VMEM((16, N), jnp.float32), half, half]
    scratch += [pltpu.VMEM((2, 8, 128), jnp.float32), pltpu.SemaphoreType.DMA((5,))]
    args = [field, t["twist_y"], t["w1"], slow]
    return call(forward_y, [shape(LAT * FIRST, 128)], scratch, args, large=(0, 1, 2, 3))[0]


def phase_tables(freq, refslow, lat, t):
    args = [freq, refslow, lat, t["x"], t["twist_x"], t["edge"], t["gather"]]
    outs = [shape(2, 256, 128)] + [jax.ShapeDtypeStruct(a.shape, a.dtype) for a in args[3:]]
    return call(phases, outs, [pltpu.SemaphoreType.DMA((4,))], args, scalars=(0, 1, 2), large=(3, 4, 5, 6))


def continue_x(block, tabs):
    scratch = [pltpu.VMEM((256, 256), jnp.bfloat16)] * 2
    return call(along_x, [shape(LAT * SECOND, 128)], scratch, [block, *tabs])[0]


def correction_tables(freq, refslow, classes, coupling, last, slow, blocks, t):
    half = jnp.bfloat16
    outs = [shape(2, 32, N), shape(8, N), shape(2, 8, 64, 256, dtype=half), shape(2, 8, 64, 256, dtype=half)]
    scratch = [pltpu.VMEM((2, 2, 16, 64, 128), half)]
    args = [freq, refslow, classes, coupling, last, slow, blocks, t["own"], t["spread"]]
    return call(weights, outs, scratch, args, scalars=(0, 1, 2, 3, 4))


def correct(block, tabs, fresh, t):
    plane = pltpu.VMEM((2, 32, N), jnp.float32)
    scratch = [pltpu.VMEM((320, 256), jnp.float32), pltpu.VMEM((2, 48, N), jnp.float32)]
    scratch += [plane, plane, plane, pltpu.SemaphoreType.DMA]
    args = [block, t["w3"], t["twist_y"], *tabs, t["own"], t["fold"], fresh]
    return call(finish, [shape(2, 32, N), shape(32, N)], scratch, args, large=(9,))


def exchange(block):
    blocks = block.reshape(LAT, 1, -1)
    return lax.all_to_all(blocks, "lat", split_axis=0, concat_axis=0, tiled=True).reshape(block.shape)


def after(value, *others):
    return lax.optimization_barrier((value, others))


def per_device(
    field, fresh, freq_index, ref_slowness, slowness, tile_classes, fd_blocks, fd_coupling, image
):
    t = tables()
    slow = slowness[0]
    block = spread_y(field.reshape(2, 32, N), slow, t)
    block, (freq, refslow, blocks) = after(block, freq_index.reshape(1), ref_slowness, fd_blocks)
    received = exchange(block)
    lat = lax.axis_index("lat").reshape(1).astype(jnp.int32)
    block = continue_x(received, phase_tables(freq, refslow, lat, t))
    block, (freq, classes, slow) = after(block, freq, tile_classes.reshape(32), slow)
    received = exchange(block)
    count = lax.axis_size("depth")
    last = (lax.axis_index("depth") == count - 1).reshape(1).astype(jnp.int32)
    blocks = jnp.stack([blocks, jnp.swapaxes(blocks, 2, 3)]).reshape(2048, 32)
    tabs = correction_tables(freq, refslow, classes, fd_coupling.reshape(32), last, slow, blocks, t)
    result, real = correct(received, tabs, fresh[0], t)
    next_field = lax.ppermute(result, "depth", [(i, (i + 1) % count) for i in range(count)])
    return next_field[None, None], image + real[None]


def solution(mesh):
    return jax.shard_map(
        per_device,
        mesh=mesh,
        in_specs=(
            P("depth", None, None, "lat", None),
            P(None, None, "lat", None),
            P("depth", None),
            P("depth"),
            P("depth", "lat", None),
            P("depth", "lat", None),
            P(),
            P(),
            P("depth", "lat", None),
        ),
        out_specs=(P("depth", None, None, "lat", None), P("depth", "lat", None)),
        check_vma=False,
    )
```

```python
import math

import jax
import jax.numpy as jnp
import ml_dtypes
import numpy as np
from jax import lax
from jax.experimental import pallas as pl
from jax.experimental.pallas import tpu as pltpu
from jax.sharding import PartitionSpec as P

LOW_HZ = 5.0
STEP_HZ = 0.25
DEPTH_KM = 0.01
SPACING_KM = 0.025
N = 1024
LAT = 32
NORM = 1.0 / (N * N)
INTERPRET = False


def parts(values):
    high = values.astype(ml_dtypes.bfloat16)
    low = (values - high.astype(np.float64)).astype(ml_dtypes.bfloat16)
    return np.stack([high, low])


def rotation(angle):
    cos, sin = np.cos(angle), np.sin(angle)
    return np.stack([np.stack([cos, -sin]), np.stack([sin, cos])])


def tables():
    n2 = np.arange(128)
    small = np.arange(32)
    k2 = np.arange(128).reshape(32, 4)
    line = rotation(-2 * np.pi * (k2[:, :, None] * n2 % 128) / 128)
    w1 = line.transpose(2, 0, 3, 1, 4).reshape(256, 256)
    line = rotation(2 * np.pi * (k2[:, :, None] * n2 % 128) / 128)
    w3 = line.transpose(2, 1, 3, 0, 4).reshape(256, 256)
    grid = 2 * np.pi * (small[:, None] * small % 32) / 32
    eye4 = np.eye(4)
    peers = []
    for sign in (-1, 1):
        high, low = parts(rotation(sign * grid).transpose(0, 2, 1, 3).reshape(64, 64))
        peers.append(np.concatenate([high, high, low], axis=1))
    b1 = np.einsum("dcxp,kl->ckxdlp", rotation(-grid), eye4).reshape(256, 256)
    b2 = np.einsum("dcpx,kl->ckpdlx", rotation(grid), eye4).reshape(256, 256)
    ty = 2 * np.pi * np.arange(8)[:, None] * n2 / N
    tx = np.tile(2 * np.pi * small[:, None] * small / N, (1, 4))
    twist_y = np.stack([np.cos(ty), np.sin(ty)]).astype(np.float32)
    twist_x = np.stack([np.cos(tx), np.sin(tx)]).astype(np.float32)
    fold = np.zeros((4, 8, 2, 2, 16, 8))
    for k1 in range(8):
        for side in range(2):
            fold[k1 % 4, :, k1 // 4, side, k1, side] = 1
    fold = fold.reshape(128, 128).astype(ml_dtypes.bfloat16)
    own = (np.arange(128)[None, :] // 32 == np.arange(4)[:, None]).astype(np.float32)
    own = np.broadcast_to(np.tile(own, (1, 2))[:, None, :], (4, 32, 256)).astype(ml_dtypes.bfloat16)
    spread = np.tile(np.eye(32), (1, 4)).astype(ml_dtypes.bfloat16)
    return {
        "w1": parts(w1),
        "w3": parts(w3),
        "x": np.stack([parts(b1), parts(b2)]),
        "peers": np.stack(peers),
        "twist_y": twist_y,
        "twist_x": twist_x,
        "fold": fold,
        "own": own,
        "spread": spread,
    }


NN = (((1,), (0,)), ((), ()))
NT = (((1,), (1,)), ((), ()))


def split(values):
    high = values.astype(jnp.bfloat16)
    low = (values - high.astype(jnp.float32)).astype(jnp.bfloat16)
    return high, low


def product(left, right, dims=NN):
    dot = lambda a, b: lax.dot_general(a, b, dims, preferred_element_type=jnp.float32)
    rows = left[0].shape[0]
    both = dot(jnp.concatenate(left, axis=0), right[0])
    return both[:rows] + (both[rows:] + dot(left[0], right[1]))


def cmul(a, b):
    return a[0] * b[0] - a[1] * b[1], a[0] * b[1] + a[1] * b[0]


def dft(values, sign):
    count = len(values)
    if count == 1:
        return values
    even, odd = dft(values[0::2], sign), dft(values[1::2], sign)
    first, second = [], []
    for k in range(count // 2):
        re, im = odd[k]
        if 4 * k == count:
            re, im = -sign * im, sign * re
        elif k:
            cos = math.cos(2 * math.pi * k / count)
            sin = sign * math.sin(2 * math.pi * k / count)
            if 8 * k == count:
                re, im = cos * (re - sign * im), cos * (im + sign * re)
            else:
                re, im = cmul(odd[k], (cos, sin))
        first.append((even[k][0] + re, even[k][1] + im))
        second.append((even[k][0] - re, even[k][1] - im))
    return first + second


def call(body, outs, scratch, args, scalars=(), large=()):
    size = sum(math.prod(o.shape) * o.dtype.itemsize for o in outs)
    size += sum(math.prod(a.shape) * a.dtype.itemsize for a in args)
    args = [pltpu.with_memory_space_constraint(a, pltpu.HBM) if i in large else a for i, a in enumerate(args)]
    space = lambda i: pltpu.SMEM if i in scalars else pltpu.HBM if i in large else pltpu.VMEM
    return pl.pallas_call(
        body,
        out_shape=outs,
        in_specs=[pl.BlockSpec(memory_space=space(i)) for i in range(len(args))],
        out_specs=[pl.BlockSpec(memory_space=pltpu.VMEM) for _ in outs],
        scratch_shapes=scratch,
        compiler_params=pltpu.CompilerParams(vmem_limit_bytes=24 << 20),
        cost_estimate=pl.CostEstimate(flops=0, bytes_accessed=size, transcendentals=0),
        interpret=INTERPRET,
    )(*args)


def fetch(sources, targets, sems):
    copies = [pltpu.make_async_copy(a, b, sems.at[i]) for i, (a, b) in enumerate(zip(sources, targets, strict=True))]
    for copy in copies:
        copy.start()
    return copies


def shape(*dims, dtype=jnp.float32):
    return jax.ShapeDtypeStruct(dims, dtype)


FIRST = 17
SECOND = 18


def lane_of(dims):
    return lax.broadcasted_iota(jnp.int32, dims, len(dims) - 1)


def forward_y(
    field_any, twist_any, w1_any, slow_any, out_ref,
    field_ref, twist_ref, w1_ref, slow_ref, high_ref, low_ref, ends_ref, sems,
):
    sources = [field_any, twist_any, slow_any.at[0:8], slow_any.at[24:32], w1_any]
    copies = fetch(sources, [field_ref, twist_ref, slow_ref.at[0:8], slow_ref.at[8:16], w1_ref], sems)
    copies[0].wait()
    copies[1].wait()
    for top in range(0, 32, 16):
        rows = slice(top, top + 16)
        lines = [
            tuple(field_ref[c, rows, n1 * 128 : n1 * 128 + 128] for c in range(2)) for n1 in range(8)
        ]
        for k1, value in enumerate(dft(lines, -1)):
            if k1:
                cos, sin = twist_ref[0, k1 : k1 + 1], twist_ref[1, k1 : k1 + 1]
                value = cmul(value, (cos, -sin))
            at = slice(k1 * 32 + top, k1 * 32 + top + 16)
            for c in range(2):
                high, low = split(value[c])
                high_ref[at, c * 128 : c * 128 + 128] = high
                low_ref[at, c * 128 : c * 128 + 128] = low
    copies[2].wait()
    copies[3].wait()
    for n1 in range(8):
        ends_ref[0, n1 : n1 + 1] = slow_ref[0:1, n1 * 128 : n1 * 128 + 128]
        ends_ref[1, n1 : n1 + 1] = slow_ref[15:16, n1 * 128 : n1 * 128 + 128]
    lane = lane_of((8, 128))
    for m in range(4):
        first = pltpu.roll(ends_ref[0], (-32 * m) % 128, 1)
        last = pltpu.roll(ends_ref[1], (32 - 32 * m) % 128, 1)
        out_ref[pl.ds(FIRST * m + 16, 8, stride=4 * FIRST), :] = jnp.where(lane < 32, first, last)
    copies[4].wait()
    out = product((w1_ref[0], w1_ref[1]), (high_ref[...], low_ref[...]), NT)
    for j in range(LAT):
        for half in range(2):
            top = FIRST * j + half * 8
            out_ref[top : top + 8] = out[j * 8 : j * 8 + 8, half * 128 : half * 128 + 128]


def sincos(angle):
    return jnp.cos(angle), jnp.sin(angle)


def phases(freq_ref, slow_ref, lat_ref, x_any, peers_any, twist_any, out_ref, x_ref, peers_ref, twist_ref, sems):
    copies = fetch([x_any, peers_any, twist_any], [x_ref, peers_ref, twist_ref], sems)
    omega = 2.0 * math.pi * (LOW_HZ + STEP_HZ * freq_ref[0].astype(jnp.float32))
    reach = omega * slow_ref[0]
    scale = 2.0 * math.pi / (N * SPACING_KM)
    for block in range(8):
        h, k2l = block // 4, block % 4
        q = lax.broadcasted_iota(jnp.int32, (32, 128), 0)
        lane = lax.broadcasted_iota(jnp.int32, (32, 128), 1)
        kx = q + 32 * (lane % 32)
        ky = h * 4 + lane // 32 + 8 * (4 * lat_ref[0] + k2l)
        kx = jnp.where(kx < N // 2, kx, kx - N).astype(jnp.float32) * scale
        ky = jnp.where(ky < N // 2, ky, ky - N).astype(jnp.float32) * scale
        square = reach * reach - kx * kx - ky * ky
        root = jnp.sqrt(jnp.abs(square))
        angle = jnp.where(square > 0, root * DEPTH_KM, 0.0)
        amplitude = jnp.where(square > 0, 1.0, jnp.exp(-root * DEPTH_KM))
        cos, sin = sincos(angle)
        out_ref[0, block * 32 : block * 32 + 32] = amplitude * cos
        out_ref[1, block * 32 : block * 32 + 32] = amplitude * sin
    for copy in copies:
        copy.wait()


def both_tiles(ref, rows):
    return [
        jnp.concatenate([ref[rows * i + half * 8 : rows * i + half * 8 + 8] for i in range(LAT)], axis=0) for half in range(2)
    ]


def along_x(in_ref, phase_ref, x_ref, peers_ref, twist_ref, out_ref, high_ref, low_ref, back_ref):
    dot = lambda a, b: lax.dot_general(a, b, NN, preferred_element_type=jnp.float32)
    blocks = [(h, k2l) for h in range(2) for k2l in range(4)]
    lines = jnp.concatenate(
        [
            jnp.concatenate([in_ref[pl.ds(h * 8 + c * 4 + k2l, LAT, stride=FIRST), :] for h, k2l in blocks], axis=1)
            for c in range(2)
        ],
        axis=0,
    )
    high, low = split(lines)
    mixed = dot(peers_ref[0], jnp.concatenate([high, low, high], axis=0))
    cos, sin = twist_ref[0], twist_ref[1]

    def put(at, value):
        for c in range(2):
            high, low = split(value[c])
            high_ref[at, c * 128 : c * 128 + 128] = high
            low_ref[at, c * 128 : c * 128 + 128] = low

    for block in range(8):
        lanes = slice(block * 128, block * 128 + 128)
        put(slice(block * 32, block * 32 + 32), cmul((mixed[:32, lanes], mixed[32:, lanes]), (cos, -sin)))
    spectrum = product((high_ref[...], low_ref[...]), (x_ref[0, 0], x_ref[0, 1]))
    for block in range(8):
        rows = slice(block * 32, block * 32 + 32)
        value = (spectrum[rows, :128], spectrum[rows, 128:])
        put(rows, cmul(value, (phase_ref[0, rows], phase_ref[1, rows])))
    mixed = product((high_ref[...], low_ref[...]), (x_ref[1, 0], x_ref[1, 1]))
    for block in range(8):
        rows, lanes = slice(block * 32, block * 32 + 32), slice(block * 128, block * 128 + 128)
        value = cmul((mixed[rows, :128], mixed[rows, 128:]), (cos, sin))
        for c in range(2):
            high, low = split(value[c])
            for at, piece in enumerate((high, low, high)):
                back_ref[at * 64 + c * 32 : at * 64 + c * 32 + 32, lanes] = piece
    out = dot(peers_ref[1], back_ref[...])
    lane, row = lane_of((LAT, 128)), lax.broadcasted_iota(jnp.int32, (LAT, 128), 0)
    edge = jnp.zeros((LAT, 128), jnp.float32)
    for block, (h, k2l) in enumerate(blocks):
        for c in range(2):
            piece = out[c * 32 : c * 32 + 32, block * 128 : block * 128 + 128]
            out_ref[pl.ds(h * 8 + c * 4 + k2l, LAT, stride=SECOND), :] = piece
            at = (c * 4 + k2l) * 4 + h * 2
            edge = jnp.where(lane % 32 == at, pltpu.roll(piece, (at - 31) % 128, 1), edge)
            edge = jnp.where(lane % 32 == at + 1, pltpu.roll(piece, at + 1, 1), edge)
    before = jnp.where(row == 0, 0.0, pltpu.roll(edge, 1, 0))
    after = jnp.where(row == LAT - 1, 0.0, pltpu.roll(edge, LAT - 1, 0))
    out_ref[pl.ds(16, LAT, stride=SECOND), :] = jnp.where(lane % 2 == 0, before, after)
    slow = in_ref[pl.ds(16, LAT, stride=FIRST), :]
    before = pltpu.roll(pltpu.roll(slow, 96, 1), 1, 0)
    after = pltpu.roll(pltpu.roll(slow, 32, 1), LAT - 1, 0)
    out_ref[pl.ds(17, LAT, stride=SECOND), :] = jnp.where(lane < 32, before, after)


def weights(
    freq_ref, refslow_ref, class_ref, coupling_ref, last_ref, slow_ref, blocks_ref, own_ref, spread_ref,
    lens_ref, row_ref, mx_ref, my_ref, wide_ref,
):
    omega = 2.0 * math.pi * (LOW_HZ + STEP_HZ * freq_ref[0].astype(jnp.float32))
    base = refslow_ref[0]
    for top in range(0, 32, 8):
        rows = slice(top, top + 8)
        cos, sin = sincos(omega * (slow_ref[rows] - base) * DEPTH_KM)
        lens_ref[0, rows], lens_ref[1, rows] = cos * NORM, sin * NORM
    high, low = split(blocks_ref[...])
    dot = lambda a: lax.dot_general(a, spread_ref[...], NN, preferred_element_type=jnp.float32)
    wide_ref[0] = dot(high).astype(jnp.bfloat16).reshape(2, 16, 64, 128)
    wide_ref[1] = dot(low).astype(jnp.bfloat16).reshape(2, 16, 64, 128)
    row_ref[2:3] = jnp.full((1, N), omega)
    row_ref[3:4] = jnp.full((1, N), base)
    row_ref[4:5] = jnp.full((1, N), last_ref[0].astype(jnp.float32))
    lane = lax.broadcasted_iota(jnp.int32, (1, 128), 1) // 32
    for g in range(8):
        classes = [class_ref[g * 4 + t] for t in range(4)]
        for c in range(2):
            beta = jnp.full((1, 128), coupling_ref[classes[0] * 2 + c])
            for t in range(1, 4):
                beta = jnp.where(lane == t, coupling_ref[classes[t] * 2 + c], beta)
            row_ref[c : c + 1, g * 128 : g * 128 + 128] = beta
        for part in range(2):
            total = []
            for turned in range(2):
                for c in range(2):
                    own = [
                        wide_ref[part, turned, classes[t], c * 32 : c * 32 + 32] * own_ref[t, :, :128] for t in range(4)
                    ]
                    total.append((own[0] + own[1]) + (own[2] + own[3]))
            mx_ref[part, g, :32, :128] = total[0]
            mx_ref[part, g, :32, 128:] = -total[1]
            mx_ref[part, g, 32:, :128] = total[1]
            mx_ref[part, g, 32:, 128:] = total[0]
            my_ref[part, g, :32, :128] = total[2]
            my_ref[part, g, :32, 128:] = total[3]
            my_ref[part, g, 32:, :128] = -total[3]
            my_ref[part, g, 32:, 128:] = total[2]


def finish(
    in_ref, w3_ref, twist_ref, lens_ref, row_ref, mx_ref, my_ref, own_ref, fold_ref, fresh_any,
    out_ref, real_ref, mixed_ref, lensed_ref, rhs_ref, across_ref, fresh_ref, sem,
):
    copy = pltpu.make_async_copy(fresh_any, fresh_ref, sem)
    copy.start()
    lane = lane_of((8, 128))
    sides = [None, None]
    for m in range(4):
        pieces = in_ref[pl.ds(17 + SECOND * m, 8, stride=4 * SECOND), :]
        for side in range(2):
            piece = pltpu.roll(pieces, (32 * m - 32 * side) % 128, 1)
            sides[side] = piece if m == 0 else jnp.where(lane // 32 == m, piece, sides[side])
    side_lens = []
    for side in range(2):
        cos, sin = sincos(row_ref[2:3, :128] * (sides[side] - row_ref[3:4, :128]) * DEPTH_KM)
        side_lens.append((cos * NORM, sin * NORM))
    beside = jnp.concatenate(
        [jnp.broadcast_to(in_ref[SECOND * j + 16 : SECOND * j + 17], (8, 128)) for j in range(LAT)], axis=0
    )
    own = lane_of((256, 128)) % 32 // 4 == lax.broadcasted_iota(jnp.int32, (256, 128), 0) % 8
    high, low = split(jnp.where(own, beside, 0.0))
    dot = lambda a: lax.dot_general(a, fold_ref[...], NN, preferred_element_type=jnp.float32)
    lines = [*both_tiles(in_ref, SECOND), dot(high) + dot(low)]
    turned = jnp.concatenate([line.T for line in lines], axis=0)[:320]
    mixed_ref[...] = product(split(turned), (w3_ref[0], w3_ref[1]))
    for block in range(5):
        values = []
        for k1 in range(8):
            top = k1 * 32 + block * 8 if block < 4 else 256 + k1 * 8
            value = (mixed_ref[top : top + 8, :128], mixed_ref[top : top + 8, 128:])
            if k1:
                value = cmul(value, (twist_ref[0, k1 : k1 + 1], twist_ref[1, k1 : k1 + 1]))
            values.append(value)
        for n1, value in enumerate(dft(values, 1)):
            lanes = slice(n1 * 128, n1 * 128 + 128)
            rows = slice(block * 8, block * 8 + 8)
            if block < 4:
                value = cmul(value, (lens_ref[0, rows, lanes], lens_ref[1, rows, lanes]))
                for c in range(2):
                    lensed_ref[c, 8 + block * 8 : 16 + block * 8, lanes] = value[c]
                continue
            for side, at in enumerate((7, 40)):
                pair = [value[c][side : side + 1] for c in range(2)]
                pair = cmul(pair, [side_lens[side][c][n1 : n1 + 1] for c in range(2)])
                for c in range(2):
                    lensed_ref[c, at : at + 1, lanes] = pair[c]
    for g in range(0, 8, 2):
        pair = []
        for lanes in (slice(g * 128, g * 128 + 128), slice(g * 128 + 128, g * 128 + 256)):
            beta = (row_ref[0:1, lanes], row_ref[1:2, lanes])
            mid = [lensed_ref[c, 8:40, lanes] for c in range(2)]
            diff = tuple(
                lensed_ref[c, 9:41, lanes] + lensed_ref[c, 7:39, lanes] - 2.0 * mid[c] for c in range(2)
            )
            more = cmul(diff, beta)
            pair.append([split(mid[c] + more[c]) for c in range(2)])
        rhs = [
            jnp.concatenate(
                [
                    jnp.concatenate([pieces[c][part] * own_ref[t, :, :128] for pieces in pair], axis=1)
                    for c in range(2)
                    for t in range(4)
                ],
                axis=0,
            )
            for part in range(2)
        ]
        left = [jnp.concatenate([mx_ref[part, g], mx_ref[part, g + 1]], axis=0) for part in range(2)]
        out = product(left, rhs)
        for c in range(2):
            across_ref[c, :, g * 128 : g * 128 + 128] = out[c * 32 : c * 32 + 32, :128]
            across_ref[c, :, g * 128 + 128 : g * 128 + 256] = out[64 + c * 32 : 96 + c * 32, 128:]
    lane = lax.broadcasted_iota(jnp.int32, (32, N), 1)
    diff = []
    for c in range(2):
        whole = across_ref[c]
        after = jnp.where(lane == N - 1, 0.0, pltpu.roll(whole, N - 1, 1))
        before = jnp.where(lane == 0, 0.0, pltpu.roll(whole, 1, 1))
        diff.append(after + before - 2.0 * whole)
    more = cmul(diff, (row_ref[0:1], row_ref[1:2]))
    for c in range(2):
        rhs_ref[c] = across_ref[c] + more[c]
    copy.wait()
    for g in range(8):
        lanes = slice(g * 128, g * 128 + 128)
        rhs = jnp.concatenate([rhs_ref[0, :, lanes], rhs_ref[1, :, lanes]], axis=1)
        tiles = [
            jnp.concatenate(
                [my_ref[part, g, c * 32 : c * 32 + 32] * own_ref[t] for c in range(2) for t in range(4)], axis=0
            )
            for part in range(2)
        ]
        out = product(split(rhs), tiles, NN)
        real_ref[:, lanes] = out[:, :128]
        last = row_ref[4:5, lanes] > 0.5
        for c in range(2):
            out_ref[c, :, lanes] = jnp.where(last, fresh_ref[c, :, lanes], out[:, c * 128 : c * 128 + 128])


def spread_y(field, slow, t):
    half = pltpu.VMEM((256, 256), jnp.bfloat16)
    scratch = [pltpu.VMEM((2, 32, N), jnp.float32), pltpu.VMEM((2, 8, 128), jnp.float32)]
    scratch += [pltpu.VMEM((2, 256, 256), jnp.bfloat16), pltpu.VMEM((16, N), jnp.float32), half, half]
    scratch += [pltpu.VMEM((2, 8, 128), jnp.float32), pltpu.SemaphoreType.DMA((5,))]
    args = [field, t["twist_y"], t["w1"], slow]
    return call(forward_y, [shape(LAT * FIRST, 128)], scratch, args, large=(0, 1, 2, 3))[0]


def phase_tables(freq, refslow, lat, t):
    args = [freq, refslow, lat, t["x"], t["peers"], t["twist_x"]]
    outs = [shape(2, 256, 128)] + [jax.ShapeDtypeStruct(a.shape, a.dtype) for a in args[3:]]
    return call(phases, outs, [pltpu.SemaphoreType.DMA((3,))], args, scalars=(0, 1, 2), large=(3, 4, 5))


def continue_x(block, tabs):
    scratch = [pltpu.VMEM((256, 256), jnp.bfloat16)] * 2 + [pltpu.VMEM((192, N), jnp.bfloat16)]
    return call(along_x, [shape(LAT * SECOND, 128)], scratch, [block, *tabs])[0]


def correction_tables(freq, refslow, classes, coupling, last, slow, blocks, t):
    half = jnp.bfloat16
    outs = [shape(2, 32, N), shape(8, N), shape(2, 8, 64, 256, dtype=half), shape(2, 8, 64, 256, dtype=half)]
    scratch = [pltpu.VMEM((2, 2, 16, 64, 128), half)]
    args = [freq, refslow, classes, coupling, last, slow, blocks, t["own"], t["spread"]]
    return call(weights, outs, scratch, args, scalars=(0, 1, 2, 3, 4))


def correct(block, tabs, fresh, t):
    plane = pltpu.VMEM((2, 32, N), jnp.float32)
    scratch = [pltpu.VMEM((320, 256), jnp.float32), pltpu.VMEM((2, 48, N), jnp.float32)]
    scratch += [plane, plane, plane, pltpu.SemaphoreType.DMA]
    args = [block, t["w3"], t["twist_y"], *tabs, t["own"], t["fold"], fresh]
    return call(finish, [shape(2, 32, N), shape(32, N)], scratch, args, large=(9,))


def exchange(block):
    blocks = block.reshape(LAT, 1, -1)
    return lax.all_to_all(blocks, "lat", split_axis=0, concat_axis=0, tiled=True).reshape(block.shape)


def after(value, *others):
    return lax.optimization_barrier((value, others))


def per_device(
    field, fresh, freq_index, ref_slowness, slowness, tile_classes, fd_blocks, fd_coupling, image
):
    t = tables()
    slow = slowness[0]
    block = spread_y(field.reshape(2, 32, N), slow, t)
    block, (freq, refslow, blocks) = after(block, freq_index.reshape(1), ref_slowness, fd_blocks)
    received = exchange(block)
    lat = lax.axis_index("lat").reshape(1).astype(jnp.int32)
    block = continue_x(received, phase_tables(freq, refslow, lat, t))
    block, (freq, classes, slow) = after(block, freq, tile_classes.reshape(32), slow)
    received = exchange(block)
    count = lax.axis_size("depth")
    last = (lax.axis_index("depth") == count - 1).reshape(1).astype(jnp.int32)
    blocks = jnp.stack([blocks, jnp.swapaxes(blocks, 2, 3)]).reshape(2048, 32)
    tabs = correction_tables(freq, refslow, classes, fd_coupling.reshape(32), last, slow, blocks, t)
    result, real = correct(received, tabs, fresh[0], t)
    next_field = lax.ppermute(result, "depth", [(i, (i + 1) % count) for i in range(count)])
    return next_field[None, None], image + real[None]


def solution(mesh):
    return jax.shard_map(
        per_device,
        mesh=mesh,
        in_specs=(
            P("depth", None, None, "lat", None),
            P(None, None, "lat", None),
            P("depth", None),
            P("depth"),
            P("depth", "lat", None),
            P("depth", "lat", None),
            P(),
            P(),
            P("depth", "lat", None),
        ),
        out_specs=(P("depth", None, None, "lat", None), P("depth", "lat", None)),
        check_vma=False,
    )
```

```python
import math

import jax
import jax.numpy as jnp
import ml_dtypes
import numpy as np
from jax import lax
from jax.experimental import pallas as pl
from jax.experimental.pallas import tpu as pltpu
from jax.sharding import PartitionSpec as P

LOW_HZ = 5.0
STEP_HZ = 0.25
DEPTH_KM = 0.01
SPACING_KM = 0.025
N = 1024
LAT = 32
NORM = 1.0 / (N * N)
INTERPRET = False


def parts(values):
    high = values.astype(ml_dtypes.bfloat16)
    low = (values - high.astype(np.float64)).astype(ml_dtypes.bfloat16)
    return np.stack([high, low])


def rotation(angle):
    cos, sin = np.cos(angle), np.sin(angle)
    return np.stack([np.stack([cos, -sin]), np.stack([sin, cos])])


def tables():
    n2 = np.arange(128)
    small = np.arange(32)
    k2 = np.arange(128).reshape(32, 4)
    line = rotation(-2 * np.pi * (k2[:, :, None] * n2 % 128) / 128)
    w1 = line.transpose(2, 0, 3, 1, 4).reshape(256, 256)
    line = rotation(2 * np.pi * (k2[:, :, None] * n2 % 128) / 128)
    w3 = line.transpose(2, 1, 3, 0, 4).reshape(256, 256)
    grid = 2 * np.pi * (small[:, None] * small % 32) / 32
    eye4 = np.eye(4)
    peers = []
    for sign in (-1, 1):
        high, low = parts(rotation(sign * grid).transpose(0, 2, 1, 3).reshape(64, 64))
        peers.append(np.concatenate([high, high, low], axis=1))
    b1 = np.einsum("dcxp,kl->ckxdlp", rotation(-grid), eye4).reshape(256, 256)
    b2 = np.einsum("dcpx,kl->ckpdlx", rotation(grid), eye4).reshape(256, 256)
    ty = 2 * np.pi * np.arange(8)[:, None] * n2 / N
    tx = np.tile(2 * np.pi * small[:, None] * small / N, (1, 4))
    twist_y = np.stack([np.cos(ty), np.sin(ty)]).astype(np.float32)
    twist_x = np.stack([np.cos(tx), np.sin(tx)]).astype(np.float32)
    fold = np.zeros((4, 8, 2, 2, 16, 8))
    for k1 in range(8):
        for side in range(2):
            fold[k1 % 4, :, k1 // 4, side, k1, side] = 1
    fold = fold.reshape(128, 128).astype(ml_dtypes.bfloat16)
    own = (np.arange(128)[None, :] // 32 == np.arange(4)[:, None]).astype(np.float32)
    own = np.broadcast_to(np.tile(own, (1, 2))[:, None, :], (4, 32, 256)).astype(ml_dtypes.bfloat16)
    spread = np.tile(np.eye(32), (1, 4)).astype(ml_dtypes.bfloat16)
    pick = np.einsum("gh,ab,t->gahtb", np.eye(4), np.eye(32), np.ones(4)).reshape(128, 512)
    return {
        "w1": parts(w1),
        "w3": parts(w3),
        "x": np.stack([parts(b1), parts(b2)]),
        "peers": np.stack(peers),
        "twist_y": twist_y,
        "twist_x": twist_x,
        "fold": fold,
        "own": own,
        "spread": spread,
        "pick": pick.astype(ml_dtypes.bfloat16),
    }


NN = (((1,), (0,)), ((), ()))
NT = (((1,), (1,)), ((), ()))


def split(values):
    high = values.astype(jnp.bfloat16)
    low = (values - high.astype(jnp.float32)).astype(jnp.bfloat16)
    return high, low


def product(left, right, dims=NN):
    dot = lambda a, b: lax.dot_general(a, b, dims, preferred_element_type=jnp.float32)
    rows = left[0].shape[0]
    both = dot(jnp.concatenate(left, axis=0), right[0])
    return both[:rows] + (both[rows:] + dot(left[0], right[1]))


def cmul(a, b):
    return a[0] * b[0] - a[1] * b[1], a[0] * b[1] + a[1] * b[0]


def dft(values, sign):
    count = len(values)
    if count == 1:
        return values
    even, odd = dft(values[0::2], sign), dft(values[1::2], sign)
    first, second = [], []
    for k in range(count // 2):
        re, im = odd[k]
        if 4 * k == count:
            re, im = -sign * im, sign * re
        elif k:
            cos = math.cos(2 * math.pi * k / count)
            sin = sign * math.sin(2 * math.pi * k / count)
            if 8 * k == count:
                re, im = cos * (re - sign * im), cos * (im + sign * re)
            else:
                re, im = cmul(odd[k], (cos, sin))
        first.append((even[k][0] + re, even[k][1] + im))
        second.append((even[k][0] - re, even[k][1] - im))
    return first + second


def call(body, outs, scratch, args, scalars=(), large=()):
    size = sum(math.prod(o.shape) * o.dtype.itemsize for o in outs)
    size += sum(math.prod(a.shape) * a.dtype.itemsize for a in args)
    args = [pltpu.with_memory_space_constraint(a, pltpu.HBM) if i in large else a for i, a in enumerate(args)]
    space = lambda i: pltpu.SMEM if i in scalars else pltpu.HBM if i in large else pltpu.VMEM
    return pl.pallas_call(
        body,
        out_shape=outs,
        in_specs=[pl.BlockSpec(memory_space=space(i)) for i in range(len(args))],
        out_specs=[pl.BlockSpec(memory_space=pltpu.VMEM) for _ in outs],
        scratch_shapes=scratch,
        compiler_params=pltpu.CompilerParams(vmem_limit_bytes=24 << 20),
        cost_estimate=pl.CostEstimate(flops=0, bytes_accessed=size, transcendentals=0),
        interpret=INTERPRET,
    )(*args)


def fetch(sources, targets, sems):
    copies = [pltpu.make_async_copy(a, b, sems.at[i]) for i, (a, b) in enumerate(zip(sources, targets, strict=True))]
    for copy in copies:
        copy.start()
    return copies


def shape(*dims, dtype=jnp.float32):
    return jax.ShapeDtypeStruct(dims, dtype)


FIRST = 17
SECOND = 18


def lane_of(dims):
    return lax.broadcasted_iota(jnp.int32, dims, len(dims) - 1)


def forward_y(
    field_any, twist_any, w1_any, slow_any, out_ref,
    field_ref, twist_ref, w1_ref, slow_ref, high_ref, low_ref, ends_ref, sems,
):
    sources = [field_any, twist_any, slow_any.at[0:8], slow_any.at[24:32], w1_any]
    copies = fetch(sources, [field_ref, twist_ref, slow_ref.at[0:8], slow_ref.at[8:16], w1_ref], sems)
    copies[0].wait()
    copies[1].wait()
    for top in range(0, 32, 16):
        rows = slice(top, top + 16)
        lines = [
            tuple(field_ref[c, rows, n1 * 128 : n1 * 128 + 128] for c in range(2)) for n1 in range(8)
        ]
        for k1, value in enumerate(dft(lines, -1)):
            if k1:
                cos, sin = twist_ref[0, k1 : k1 + 1], twist_ref[1, k1 : k1 + 1]
                value = cmul(value, (cos, -sin))
            at = slice(k1 * 32 + top, k1 * 32 + top + 16)
            for c in range(2):
                high, low = split(value[c])
                high_ref[at, c * 128 : c * 128 + 128] = high
                low_ref[at, c * 128 : c * 128 + 128] = low
    copies[2].wait()
    copies[3].wait()
    for n1 in range(8):
        ends_ref[0, n1 : n1 + 1] = slow_ref[0:1, n1 * 128 : n1 * 128 + 128]
        ends_ref[1, n1 : n1 + 1] = slow_ref[15:16, n1 * 128 : n1 * 128 + 128]
    lane = lane_of((8, 128))
    for m in range(4):
        first = pltpu.roll(ends_ref[0], (-32 * m) % 128, 1)
        last = pltpu.roll(ends_ref[1], (32 - 32 * m) % 128, 1)
        out_ref[pl.ds(FIRST * m + 16, 8, stride=4 * FIRST), :] = jnp.where(lane < 32, first, last)
    copies[4].wait()
    out = product((w1_ref[0], w1_ref[1]), (high_ref[...], low_ref[...]), NT)
    for j in range(LAT):
        for half in range(2):
            top = FIRST * j + half * 8
            out_ref[top : top + 8] = out[j * 8 : j * 8 + 8, half * 128 : half * 128 + 128]


def sincos(angle):
    return jnp.cos(angle), jnp.sin(angle)


def prepare(
    freq_ref, refslow_ref, lat_ref, last_ref, class_ref, coupling_ref,
    blocks_any, slow_any, spread_any, pick_any, own_any, x_any, peers_any, twist_any,
    phase_ref, lens_ref, row_ref, mx_ref, my_ref, own_ref, x_ref, peers_ref, twist_ref,
    blocks_ref, slow_ref, spread_ref, pick_ref, wide_ref, sems,
):
    copies = fetch(
        [blocks_any, spread_any, pick_any, own_any, slow_any, x_any, peers_any, twist_any],
        [blocks_ref, spread_ref, pick_ref, own_ref, slow_ref, x_ref, peers_ref, twist_ref],
        sems,
    )
    omega = 2.0 * math.pi * (LOW_HZ + STEP_HZ * freq_ref[0, 0].astype(jnp.float32))
    base = refslow_ref[0]
    phases(omega * base, lat_ref[0], phase_ref)
    for copy in copies:
        copy.wait()
    for top in range(0, 32, 8):
        rows = slice(top, top + 8)
        cos, sin = sincos(omega * (slow_ref[rows] - base) * DEPTH_KM)
        lens_ref[0, rows], lens_ref[1, rows] = cos * NORM, sin * NORM
    row_ref[2:3] = jnp.full((1, N), omega)
    row_ref[3:4] = jnp.full((1, N), base)
    row_ref[4:5] = jnp.full((1, N), last_ref[0].astype(jnp.float32))
    weights(class_ref, coupling_ref, blocks_ref, spread_ref, pick_ref, own_ref, row_ref, mx_ref, my_ref, wide_ref)


def phases(reach, lat, out_ref):
    scale = 2.0 * math.pi / (N * SPACING_KM)
    for block in range(8):
        h, k2l = block // 4, block % 4
        q = lax.broadcasted_iota(jnp.int32, (32, 128), 0)
        lane = lax.broadcasted_iota(jnp.int32, (32, 128), 1)
        kx = q + 32 * (lane % 32)
        ky = h * 4 + lane // 32 + 8 * (4 * lat + k2l)
        kx = jnp.where(kx < N // 2, kx, kx - N).astype(jnp.float32) * scale
        ky = jnp.where(ky < N // 2, ky, ky - N).astype(jnp.float32) * scale
        square = reach * reach - kx * kx - ky * ky
        root = jnp.sqrt(jnp.abs(square))
        angle = jnp.where(square > 0, root * DEPTH_KM, 0.0)
        amplitude = jnp.where(square > 0, 1.0, jnp.exp(-root * DEPTH_KM))
        cos, sin = sincos(angle)
        out_ref[0, block * 32 : block * 32 + 32] = amplitude * cos
        out_ref[1, block * 32 : block * 32 + 32] = amplitude * sin


def both_tiles(ref, rows):
    return [
        jnp.concatenate([ref[rows * i + half * 8 : rows * i + half * 8 + 8] for i in range(LAT)], axis=0) for half in range(2)
    ]


def along_x(in_ref, phase_ref, x_ref, peers_ref, twist_ref, out_ref, high_ref, low_ref, back_ref):
    dot = lambda a, b: lax.dot_general(a, b, NN, preferred_element_type=jnp.float32)
    blocks = [(h, k2l) for h in range(2) for k2l in range(4)]
    lines = jnp.concatenate(
        [
            jnp.concatenate([in_ref[pl.ds(h * 8 + c * 4 + k2l, LAT, stride=FIRST), :] for h, k2l in blocks], axis=1)
            for c in range(2)
        ],
        axis=0,
    )
    high, low = split(lines)
    mixed = dot(peers_ref[0], jnp.concatenate([high, low, high], axis=0))
    cos, sin = twist_ref[0], twist_ref[1]

    def put(at, value):
        for c in range(2):
            high, low = split(value[c])
            high_ref[at, c * 128 : c * 128 + 128] = high
            low_ref[at, c * 128 : c * 128 + 128] = low

    for block in range(8):
        lanes = slice(block * 128, block * 128 + 128)
        put(slice(block * 32, block * 32 + 32), cmul((mixed[:32, lanes], mixed[32:, lanes]), (cos, -sin)))
    spectrum = product((high_ref[...], low_ref[...]), (x_ref[0, 0], x_ref[0, 1]))
    for block in range(8):
        rows = slice(block * 32, block * 32 + 32)
        value = (spectrum[rows, :128], spectrum[rows, 128:])
        put(rows, cmul(value, (phase_ref[0, rows], phase_ref[1, rows])))
    mixed = product((high_ref[...], low_ref[...]), (x_ref[1, 0], x_ref[1, 1]))
    for block in range(8):
        rows, lanes = slice(block * 32, block * 32 + 32), slice(block * 128, block * 128 + 128)
        value = cmul((mixed[rows, :128], mixed[rows, 128:]), (cos, sin))
        for c in range(2):
            high, low = split(value[c])
            for at, piece in enumerate((high, low, high)):
                back_ref[at * 64 + c * 32 : at * 64 + c * 32 + 32, lanes] = piece
    out = dot(peers_ref[1], back_ref[...])
    lane, row = lane_of((LAT, 128)), lax.broadcasted_iota(jnp.int32, (LAT, 128), 0)
    edge = jnp.zeros((LAT, 128), jnp.float32)
    for block, (h, k2l) in enumerate(blocks):
        for c in range(2):
            piece = out[c * 32 : c * 32 + 32, block * 128 : block * 128 + 128]
            out_ref[pl.ds(h * 8 + c * 4 + k2l, LAT, stride=SECOND), :] = piece
            at = (c * 4 + k2l) * 4 + h * 2
            edge = jnp.where(lane % 32 == at, pltpu.roll(piece, (at - 31) % 128, 1), edge)
            edge = jnp.where(lane % 32 == at + 1, pltpu.roll(piece, at + 1, 1), edge)
    before = jnp.where(row == 0, 0.0, pltpu.roll(edge, 1, 0))
    after = jnp.where(row == LAT - 1, 0.0, pltpu.roll(edge, LAT - 1, 0))
    out_ref[pl.ds(16, LAT, stride=SECOND), :] = jnp.where(lane % 2 == 0, before, after)
    slow = in_ref[pl.ds(16, LAT, stride=FIRST), :]
    before = pltpu.roll(pltpu.roll(slow, 96, 1), 1, 0)
    after = pltpu.roll(pltpu.roll(slow, 32, 1), LAT - 1, 0)
    out_ref[pl.ds(17, LAT, stride=SECOND), :] = jnp.where(lane < 32, before, after)


def weights(class_ref, coupling_ref, blocks_ref, spread_ref, pick_ref, own_ref, row_ref, mx_ref, my_ref, wide_ref):
    dot = lambda a, b, dims=NN: lax.dot_general(a, b, dims, preferred_element_type=jnp.float32).astype(jnp.bfloat16)
    for part, values in enumerate(split(blocks_ref[...])):
        wide_ref[part, 0] = dot(values, spread_ref[...]).reshape(16, 64, 128)
        turned = dot(spread_ref[:, :32], values, NT)
        turned = jnp.concatenate([turned[:, k * 128 : k * 128 + 128] for k in range(8)], axis=0)
        turned = dot(turned, pick_ref[...])
        for k in range(16):
            for c in range(2):
                m = k % 2 * 2 + c
                piece = turned[k // 2 * 32 : k // 2 * 32 + 32, m * 128 : m * 128 + 128]
                wide_ref[part, 1, k, c * 32 : c * 32 + 32] = piece
    lane = lax.broadcasted_iota(jnp.int32, (1, 128), 1) // 32
    for g in range(8):
        classes = [class_ref[0, 0, g * 4 + t] for t in range(4)]
        for c in range(2):
            beta = jnp.full((1, 128), coupling_ref[classes[0], c])
            for t in range(1, 4):
                beta = jnp.where(lane == t, coupling_ref[classes[t], c], beta)
            row_ref[c : c + 1, g * 128 : g * 128 + 128] = beta
        for part in range(2):
            total = []
            for turned in range(2):
                for c in range(2):
                    own = [
                        wide_ref[part, turned, classes[t], c * 32 : c * 32 + 32] * own_ref[t, :, :128] for t in range(4)
                    ]
                    total.append((own[0] + own[1]) + (own[2] + own[3]))
            mx_ref[part, g, :32, :128] = total[0]
            mx_ref[part, g, :32, 128:] = -total[1]
            mx_ref[part, g, 32:, :128] = total[1]
            mx_ref[part, g, 32:, 128:] = total[0]
            my_ref[part, g, :32, :128] = total[2]
            my_ref[part, g, :32, 128:] = total[3]
            my_ref[part, g, 32:, :128] = -total[3]
            my_ref[part, g, 32:, 128:] = total[2]


def finish(
    in_ref, w3_ref, twist_ref, lens_ref, row_ref, mx_ref, my_ref, own_ref, fold_ref, fresh_any,
    out_ref, real_ref, mixed_ref, lensed_ref, rhs_ref, across_ref, fresh_ref, sem,
):
    copy = pltpu.make_async_copy(fresh_any, fresh_ref, sem)
    copy.start()
    lane = lane_of((8, 128))
    sides = [None, None]
    for m in range(4):
        pieces = in_ref[pl.ds(17 + SECOND * m, 8, stride=4 * SECOND), :]
        for side in range(2):
            piece = pltpu.roll(pieces, (32 * m - 32 * side) % 128, 1)
            sides[side] = piece if m == 0 else jnp.where(lane // 32 == m, piece, sides[side])
    side_lens = []
    for side in range(2):
        cos, sin = sincos(row_ref[2:3, :128] * (sides[side] - row_ref[3:4, :128]) * DEPTH_KM)
        side_lens.append((cos * NORM, sin * NORM))
    beside = jnp.concatenate(
        [jnp.broadcast_to(in_ref[SECOND * j + 16 : SECOND * j + 17], (8, 128)) for j in range(LAT)], axis=0
    )
    own = lane_of((256, 128)) % 32 // 4 == lax.broadcasted_iota(jnp.int32, (256, 128), 0) % 8
    high, low = split(jnp.where(own, beside, 0.0))
    dot = lambda a: lax.dot_general(a, fold_ref[...], NN, preferred_element_type=jnp.float32)
    lines = [*both_tiles(in_ref, SECOND), dot(high) + dot(low)]
    turned = jnp.concatenate([line.T for line in lines], axis=0)[:320]
    mixed_ref[...] = product(split(turned), (w3_ref[0], w3_ref[1]))
    for block in range(5):
        values = []
        for k1 in range(8):
            top = k1 * 32 + block * 8 if block < 4 else 256 + k1 * 8
            value = (mixed_ref[top : top + 8, :128], mixed_ref[top : top + 8, 128:])
            if k1:
                value = cmul(value, (twist_ref[0, k1 : k1 + 1], twist_ref[1, k1 : k1 + 1]))
            values.append(value)
        for n1, value in enumerate(dft(values, 1)):
            lanes = slice(n1 * 128, n1 * 128 + 128)
            rows = slice(block * 8, block * 8 + 8)
            if block < 4:
                value = cmul(value, (lens_ref[0, rows, lanes], lens_ref[1, rows, lanes]))
                for c in range(2):
                    lensed_ref[c, 8 + block * 8 : 16 + block * 8, lanes] = value[c]
                continue
            for side, at in enumerate((7, 40)):
                pair = [value[c][side : side + 1] for c in range(2)]
                pair = cmul(pair, [side_lens[side][c][n1 : n1 + 1] for c in range(2)])
                for c in range(2):
                    lensed_ref[c, at : at + 1, lanes] = pair[c]
    for g in range(0, 8, 2):
        pair = []
        for lanes in (slice(g * 128, g * 128 + 128), slice(g * 128 + 128, g * 128 + 256)):
            beta = (row_ref[0:1, lanes], row_ref[1:2, lanes])
            mid = [lensed_ref[c, 8:40, lanes] for c in range(2)]
            diff = tuple(
                lensed_ref[c, 9:41, lanes] + lensed_ref[c, 7:39, lanes] - 2.0 * mid[c] for c in range(2)
            )
            more = cmul(diff, beta)
            pair.append([split(mid[c] + more[c]) for c in range(2)])
        rhs = [
            jnp.concatenate(
                [
                    jnp.concatenate([pieces[c][part] * own_ref[t, :, :128] for pieces in pair], axis=1)
                    for c in range(2)
                    for t in range(4)
                ],
                axis=0,
            )
            for part in range(2)
        ]
        left = [jnp.concatenate([mx_ref[part, g], mx_ref[part, g + 1]], axis=0) for part in range(2)]
        out = product(left, rhs)
        for c in range(2):
            across_ref[c, :, g * 128 : g * 128 + 128] = out[c * 32 : c * 32 + 32, :128]
            across_ref[c, :, g * 128 + 128 : g * 128 + 256] = out[64 + c * 32 : 96 + c * 32, 128:]
    lane = lax.broadcasted_iota(jnp.int32, (32, N), 1)
    diff = []
    for c in range(2):
        whole = across_ref[c]
        after = jnp.where(lane == N - 1, 0.0, pltpu.roll(whole, N - 1, 1))
        before = jnp.where(lane == 0, 0.0, pltpu.roll(whole, 1, 1))
        diff.append(after + before - 2.0 * whole)
    more = cmul(diff, (row_ref[0:1], row_ref[1:2]))
    for c in range(2):
        rhs_ref[c] = across_ref[c] + more[c]
    copy.wait()
    for g in range(8):
        lanes = slice(g * 128, g * 128 + 128)
        rhs = jnp.concatenate([rhs_ref[0, :, lanes], rhs_ref[1, :, lanes]], axis=1)
        tiles = [
            jnp.concatenate(
                [my_ref[part, g, c * 32 : c * 32 + 32] * own_ref[t] for c in range(2) for t in range(4)], axis=0
            )
            for part in range(2)
        ]
        out = product(split(rhs), tiles, NN)
        real_ref[:, lanes] = out[:, :128]
        last = row_ref[4:5, lanes] > 0.5
        for c in range(2):
            out_ref[c, :, lanes] = jnp.where(last, fresh_ref[c, :, lanes], out[:, c * 128 : c * 128 + 128])


def spread_y(field, slow, t):
    half = pltpu.VMEM((256, 256), jnp.bfloat16)
    scratch = [pltpu.VMEM((2, 32, N), jnp.float32), pltpu.VMEM((2, 8, 128), jnp.float32)]
    scratch += [pltpu.VMEM((2, 256, 256), jnp.bfloat16), pltpu.VMEM((16, N), jnp.float32), half, half]
    scratch += [pltpu.VMEM((2, 8, 128), jnp.float32), pltpu.SemaphoreType.DMA((5,))]
    args = [field, t["twist_y"], t["w1"], slow]
    return call(forward_y, [shape(LAT * FIRST, 128)], scratch, args, large=(0, 1, 2, 3))[0]


def prepared(freq, refslow, lat, last, classes, coupling, blocks, slow, t):
    half = jnp.bfloat16
    tables = [t["spread"], t["pick"], t["own"], t["x"], t["peers"], t["twist_x"]]
    args = [freq, refslow, lat, last, classes, coupling, blocks, slow, *tables]
    outs = [shape(2, 256, 128), shape(2, 32, N), shape(8, N)] + [shape(2, 8, 64, 256, dtype=half)] * 2
    outs += [jax.ShapeDtypeStruct(a.shape, a.dtype) for a in tables[2:]]
    scratch = [pltpu.VMEM((1024, 32), jnp.float32), pltpu.VMEM((32, N), jnp.float32), pltpu.VMEM((32, 128), half)]
    scratch += [pltpu.VMEM((128, 512), half), pltpu.VMEM((2, 2, 16, 64, 128), half), pltpu.SemaphoreType.DMA((8,))]
    phase, lens, rows, mx, my, own, x, peers, twist = call(
        prepare, outs, scratch, args, scalars=range(6), large=range(6, 14)
    )
    return [phase, x, peers, twist], [lens, rows, mx, my, own]


def continue_x(block, tabs):
    scratch = [pltpu.VMEM((256, 256), jnp.bfloat16)] * 2 + [pltpu.VMEM((192, N), jnp.bfloat16)]
    return call(along_x, [pltpu.VMEM((LAT * SECOND, 128), jnp.float32)], scratch, [block, *tabs])[0]


def correct(block, tabs, fresh, t):
    plane = pltpu.VMEM((2, 32, N), jnp.float32)
    scratch = [pltpu.VMEM((320, 256), jnp.float32), pltpu.VMEM((2, 48, N), jnp.float32)]
    scratch += [plane, plane, plane, pltpu.SemaphoreType.DMA]
    args = [block, t["w3"], t["twist_y"], *tabs, t["fold"], fresh]
    return call(finish, [shape(2, 32, N), shape(32, N)], scratch, args, large=(9,))


def exchange(block):
    blocks = block.reshape(LAT, 1, -1)
    return lax.all_to_all(blocks, "lat", split_axis=0, concat_axis=0, tiled=True).reshape(block.shape)


def after(value, *others):
    return lax.optimization_barrier((value, others))


def per_device(
    field, fresh, freq_index, ref_slowness, slowness, tile_classes, fd_blocks, fd_coupling, image
):
    t = tables()
    slow = slowness[0]
    block = spread_y(field.reshape(2, 32, N), slow, t)
    block, (blocks, slow) = after(block, fd_blocks.reshape(1024, 32), slow)
    received = exchange(block)
    lat = lax.axis_index("lat").reshape(1).astype(jnp.int32)
    count = lax.axis_size("depth")
    last = (lax.axis_index("depth") == count - 1).reshape(1).astype(jnp.int32)
    phase, tabs = prepared(freq_index, ref_slowness, lat, last, tile_classes, fd_coupling, blocks, slow, t)
    received, (phase, tabs) = after(received, phase, tabs)
    received = exchange(continue_x(received, phase))
    result, real = correct(received, tabs, fresh[0], t)
    next_field = lax.ppermute(result, "depth", [(i, (i + 1) % count) for i in range(count)])
    return next_field[None, None], image + real[None]


def solution(mesh):
    return jax.shard_map(
        per_device,
        mesh=mesh,
        in_specs=(
            P("depth", None, None, "lat", None),
            P(None, None, "lat", None),
            P("depth", None),
            P("depth"),
            P("depth", "lat", None),
            P("depth", "lat", None),
            P(),
            P(),
            P("depth", "lat", None),
        ),
        out_specs=(P("depth", None, None, "lat", None), P("depth", "lat", None)),
        check_vma=False,
    )
```

```python
import math

import jax
import jax.numpy as jnp
import ml_dtypes
import numpy as np
from jax import lax
from jax.experimental import pallas as pl
from jax.experimental.pallas import tpu as pltpu
from jax.sharding import PartitionSpec as P

LOW_HZ = 5.0
STEP_HZ = 0.25
DEPTH_KM = 0.01
SPACING_KM = 0.025
N = 1024
LAT = 32
NORM = 1.0 / (N * N)
INTERPRET = False


def parts(values):
    high = values.astype(ml_dtypes.bfloat16)
    low = (values - high.astype(np.float64)).astype(ml_dtypes.bfloat16)
    return np.stack([high, low])


def rotation(angle):
    cos, sin = np.cos(angle), np.sin(angle)
    return np.stack([np.stack([cos, -sin]), np.stack([sin, cos])])


def tables():
    n2 = np.arange(128)
    small = np.arange(32)
    k2 = np.arange(128).reshape(32, 4)
    line = rotation(-2 * np.pi * (k2[:, :, None] * n2 % 128) / 128)
    w1 = line.transpose(2, 0, 3, 1, 4).reshape(256, 256)
    line = rotation(2 * np.pi * (k2[:, :, None] * n2 % 128) / 128)
    w3 = line.transpose(2, 1, 3, 0, 4).reshape(256, 256)
    grid = 2 * np.pi * (small[:, None] * small % 32) / 32
    eye4 = np.eye(4)
    peers = []
    for sign in (-1, 1):
        high, low = parts(rotation(sign * grid).transpose(0, 2, 1, 3).reshape(64, 64))
        peers.append(np.concatenate([high, high, low], axis=1))
    b1 = np.einsum("dcxp,kl->ckxdlp", rotation(-grid), eye4).reshape(256, 256)
    b2 = np.einsum("dcpx,kl->ckpdlx", rotation(grid), eye4).reshape(256, 256)
    ty = 2 * np.pi * np.arange(8)[:, None] * n2 / N
    tx = np.tile(2 * np.pi * small[:, None] * small / N, (1, 4))
    twist_y = np.stack([np.cos(ty), np.sin(ty)]).astype(np.float32)
    twist_x = np.stack([np.cos(tx), np.sin(tx)]).astype(np.float32)
    own = (np.arange(128)[None, :] // 32 == np.arange(4)[:, None]).astype(np.float32)
    own = np.broadcast_to(np.tile(own, (1, 2))[:, None, :], (4, 32, 256)).astype(ml_dtypes.bfloat16)
    spread = np.tile(np.eye(32), (1, 4)).astype(ml_dtypes.bfloat16)
    pick = np.einsum("gh,ab,t->gahtb", np.eye(4), np.eye(32), np.ones(4)).reshape(128, 512)
    return {
        "w1": parts(w1),
        "w3": parts(w3),
        "x": np.stack([parts(b1), parts(b2)]),
        "peers": np.stack(peers),
        "twist_y": twist_y,
        "twist_x": twist_x,
        "own": own,
        "spread": spread,
        "pick": pick.astype(ml_dtypes.bfloat16),
    }


NN = (((1,), (0,)), ((), ()))
NT = (((1,), (1,)), ((), ()))


def split(values):
    high = values.astype(jnp.bfloat16)
    low = (values - high.astype(jnp.float32)).astype(jnp.bfloat16)
    return high, low


def product(left, right, dims=NN):
    dot = lambda a, b: lax.dot_general(a, b, dims, preferred_element_type=jnp.float32)
    rows = left[0].shape[0]
    both = dot(jnp.concatenate(left, axis=0), right[0])
    return both[:rows] + (both[rows:] + dot(left[0], right[1]))


def cmul(a, b):
    return a[0] * b[0] - a[1] * b[1], a[0] * b[1] + a[1] * b[0]


def dft(values, sign):
    count = len(values)
    if count == 1:
        return values
    even, odd = dft(values[0::2], sign), dft(values[1::2], sign)
    first, second = [], []
    for k in range(count // 2):
        re, im = odd[k]
        if 4 * k == count:
            re, im = -sign * im, sign * re
        elif k:
            cos = math.cos(2 * math.pi * k / count)
            sin = sign * math.sin(2 * math.pi * k / count)
            if 8 * k == count:
                re, im = cos * (re - sign * im), cos * (im + sign * re)
            else:
                re, im = cmul(odd[k], (cos, sin))
        first.append((even[k][0] + re, even[k][1] + im))
        second.append((even[k][0] - re, even[k][1] - im))
    return first + second


def call(body, outs, scratch, args, scalars=(), large=()):
    size = sum(math.prod(o.shape) * o.dtype.itemsize for o in outs)
    size += sum(math.prod(a.shape) * a.dtype.itemsize for a in args)
    args = [pltpu.with_memory_space_constraint(a, pltpu.HBM) if i in large else a for i, a in enumerate(args)]
    space = lambda i: pltpu.SMEM if i in scalars else pltpu.HBM if i in large else pltpu.VMEM
    return pl.pallas_call(
        body,
        out_shape=outs,
        in_specs=[pl.BlockSpec(memory_space=space(i)) for i in range(len(args))],
        out_specs=[pl.BlockSpec(memory_space=pltpu.VMEM) for _ in outs],
        scratch_shapes=scratch,
        compiler_params=pltpu.CompilerParams(vmem_limit_bytes=24 << 20),
        cost_estimate=pl.CostEstimate(flops=0, bytes_accessed=size, transcendentals=0),
        interpret=INTERPRET,
    )(*args)


def fetch(sources, targets, sems):
    copies = [pltpu.make_async_copy(a, b, sems.at[i]) for i, (a, b) in enumerate(zip(sources, targets, strict=True))]
    for copy in copies:
        copy.start()
    return copies


def shape(*dims, dtype=jnp.float32):
    return jax.ShapeDtypeStruct(dims, dtype)


FIRST = 17
SECOND = 18


def lane_of(dims):
    return lax.broadcasted_iota(jnp.int32, dims, len(dims) - 1)


def forward_y(
    field_any, twist_any, w1_any, slow_any, out_ref,
    field_ref, twist_ref, w1_ref, slow_ref, high_ref, low_ref, ends_ref, sems,
):
    sources = [field_any, twist_any, slow_any.at[0:8], slow_any.at[24:32], w1_any]
    copies = fetch(sources, [field_ref, twist_ref, slow_ref.at[0:8], slow_ref.at[8:16], w1_ref], sems)
    copies[0].wait()
    copies[1].wait()
    for top in range(0, 32, 16):
        rows = slice(top, top + 16)
        lines = [
            tuple(field_ref[c, rows, n1 * 128 : n1 * 128 + 128] for c in range(2)) for n1 in range(8)
        ]
        for k1, value in enumerate(dft(lines, -1)):
            if k1:
                cos, sin = twist_ref[0, k1 : k1 + 1], twist_ref[1, k1 : k1 + 1]
                value = cmul(value, (cos, -sin))
            at = slice(k1 * 32 + top, k1 * 32 + top + 16)
            for c in range(2):
                high, low = split(value[c])
                high_ref[at, c * 128 : c * 128 + 128] = high
                low_ref[at, c * 128 : c * 128 + 128] = low
    copies[2].wait()
    copies[3].wait()
    for n1 in range(8):
        ends_ref[0, n1 : n1 + 1] = slow_ref[0:1, n1 * 128 : n1 * 128 + 128]
        ends_ref[1, n1 : n1 + 1] = slow_ref[15:16, n1 * 128 : n1 * 128 + 128]
    lane = lane_of((8, 128))
    for m in range(4):
        first = pltpu.roll(ends_ref[0], (-32 * m) % 128, 1)
        last = pltpu.roll(ends_ref[1], (32 - 32 * m) % 128, 1)
        out_ref[pl.ds(FIRST * m + 16, 8, stride=4 * FIRST), :] = jnp.where(lane < 32, first, last)
    copies[4].wait()
    for first in range(0, LAT, 16):
        rows = slice(first * 8, first * 8 + 128)
        out = product((w1_ref[0, rows], w1_ref[1, rows]), (high_ref[...], low_ref[...]), NT)
        for j in range(16):
            for half in range(2):
                top = FIRST * (first + j) + half * 8
                out_ref[top : top + 8] = out[j * 8 : j * 8 + 8, half * 128 : half * 128 + 128]


def sincos(angle):
    return jnp.cos(angle), jnp.sin(angle)


def prepare(
    freq_ref, refslow_ref, lat_ref, last_ref, class_ref, coupling_ref,
    blocks_any, slow_any, spread_any, pick_any, own_any, x_any, peers_any, twist_any,
    phase_ref, lens_ref, row_ref, mx_ref, my_ref, own_ref, x_ref, peers_ref, twist_ref,
    blocks_ref, slow_ref, spread_ref, pick_ref, wide_ref, sems,
):
    copies = fetch(
        [blocks_any, spread_any, pick_any, own_any, slow_any, x_any, peers_any, twist_any],
        [blocks_ref, spread_ref, pick_ref, own_ref, slow_ref, x_ref, peers_ref, twist_ref],
        sems,
    )
    omega = 2.0 * math.pi * (LOW_HZ + STEP_HZ * freq_ref[0, 0].astype(jnp.float32))
    base = refslow_ref[0]
    phases(omega * base, lat_ref[0], phase_ref)
    for copy in copies:
        copy.wait()
    for top in range(0, 32, 8):
        rows = slice(top, top + 8)
        cos, sin = sincos(omega * (slow_ref[rows] - base) * DEPTH_KM)
        lens_ref[0, rows], lens_ref[1, rows] = cos * NORM, sin * NORM
    row_ref[2:3] = jnp.full((1, N), omega)
    row_ref[3:4] = jnp.full((1, N), base)
    row_ref[4:5] = jnp.full((1, N), last_ref[0].astype(jnp.float32))
    weights(class_ref, coupling_ref, blocks_ref, spread_ref, pick_ref, own_ref, row_ref, mx_ref, my_ref, wide_ref)


def phases(reach, lat, out_ref):
    scale = 2.0 * math.pi / (N * SPACING_KM)
    for block in range(8):
        h, k2l = block // 4, block % 4
        q = lax.broadcasted_iota(jnp.int32, (32, 128), 0)
        lane = lax.broadcasted_iota(jnp.int32, (32, 128), 1)
        kx = q + 32 * (lane % 32)
        ky = h * 4 + lane // 32 + 8 * (4 * lat + k2l)
        kx = jnp.where(kx < N // 2, kx, kx - N).astype(jnp.float32) * scale
        ky = jnp.where(ky < N // 2, ky, ky - N).astype(jnp.float32) * scale
        square = reach * reach - kx * kx - ky * ky
        root = jnp.sqrt(jnp.abs(square))
        angle = jnp.where(square > 0, root * DEPTH_KM, 0.0)
        amplitude = jnp.where(square > 0, 1.0, jnp.exp(-root * DEPTH_KM))
        cos, sin = sincos(angle)
        out_ref[0, block * 32 : block * 32 + 32] = amplitude * cos
        out_ref[1, block * 32 : block * 32 + 32] = amplitude * sin


def both_tiles(ref, rows):
    return [
        jnp.concatenate([ref[rows * i + half * 8 : rows * i + half * 8 + 8] for i in range(LAT)], axis=0) for half in range(2)
    ]


def along_x(in_ref, phase_ref, x_ref, peers_ref, twist_ref, out_ref, high_ref, low_ref, back_ref):
    dot = lambda a, b: lax.dot_general(a, b, NN, preferred_element_type=jnp.float32)
    blocks = [(h, k2l) for h in range(2) for k2l in range(4)]
    lines = jnp.concatenate(
        [
            jnp.concatenate([in_ref[pl.ds(h * 8 + c * 4 + k2l, LAT, stride=FIRST), :] for h, k2l in blocks], axis=1)
            for c in range(2)
        ],
        axis=0,
    )
    high, low = split(lines)
    mixed = dot(peers_ref[0], jnp.concatenate([high, low, high], axis=0))
    cos, sin = twist_ref[0], twist_ref[1]

    def put(at, value):
        for c in range(2):
            high, low = split(value[c])
            high_ref[at, c * 128 : c * 128 + 128] = high
            low_ref[at, c * 128 : c * 128 + 128] = low

    for half in range(2):
        some = range(half * 4, half * 4 + 4)
        whole = slice(half * 128, half * 128 + 128)
        for block in some:
            lanes = slice(block * 128, block * 128 + 128)
            put(slice(block * 32, block * 32 + 32), cmul((mixed[:32, lanes], mixed[32:, lanes]), (cos, -sin)))
        spectrum = product((high_ref[whole], low_ref[whole]), (x_ref[0, 0], x_ref[0, 1]))
        for block in some:
            rows, at = slice(block * 32, block * 32 + 32), block % 4 * 32
            value = (spectrum[at : at + 32, :128], spectrum[at : at + 32, 128:])
            put(rows, cmul(value, (phase_ref[0, rows], phase_ref[1, rows])))
        back = product((high_ref[whole], low_ref[whole]), (x_ref[1, 0], x_ref[1, 1]))
        for block in some:
            at, lanes = block % 4 * 32, slice(block * 128, block * 128 + 128)
            value = cmul((back[at : at + 32, :128], back[at : at + 32, 128:]), (cos, sin))
            for c in range(2):
                high, low = split(value[c])
                for part, piece in enumerate((high, low, high)):
                    back_ref[part * 64 + c * 32 : part * 64 + c * 32 + 32, lanes] = piece
    out = dot(peers_ref[1], back_ref[...])
    lane, row = lane_of((LAT, 128)), lax.broadcasted_iota(jnp.int32, (LAT, 128), 0)
    edge = jnp.zeros((LAT, 128), jnp.float32)
    for block, (h, k2l) in enumerate(blocks):
        for c in range(2):
            piece = out[c * 32 : c * 32 + 32, block * 128 : block * 128 + 128]
            out_ref[pl.ds(h * 8 + c * 4 + k2l, LAT, stride=SECOND), :] = piece
            at = (c * 4 + k2l) * 4 + h * 2
            edge = jnp.where(lane % 32 == at, pltpu.roll(piece, (at - 31) % 128, 1), edge)
            edge = jnp.where(lane % 32 == at + 1, pltpu.roll(piece, at + 1, 1), edge)
    before = jnp.where(row == 0, 0.0, pltpu.roll(edge, 1, 0))
    after = jnp.where(row == LAT - 1, 0.0, pltpu.roll(edge, LAT - 1, 0))
    out_ref[pl.ds(16, LAT, stride=SECOND), :] = jnp.where(lane % 2 == 0, before, after)
    slow = in_ref[pl.ds(16, LAT, stride=FIRST), :]
    before = pltpu.roll(pltpu.roll(slow, 96, 1), 1, 0)
    after = pltpu.roll(pltpu.roll(slow, 32, 1), LAT - 1, 0)
    out_ref[pl.ds(17, LAT, stride=SECOND), :] = jnp.where(lane < 32, before, after)


def weights(class_ref, coupling_ref, blocks_ref, spread_ref, pick_ref, own_ref, row_ref, mx_ref, my_ref, wide_ref):
    dot = lambda a, b, dims=NN: lax.dot_general(a, b, dims, preferred_element_type=jnp.float32).astype(jnp.bfloat16)
    for part, values in enumerate(split(blocks_ref[...])):
        wide_ref[part, 0] = dot(values, spread_ref[...]).reshape(16, 64, 128)
        turned = dot(spread_ref[:, :32], values, NT)
        turned = jnp.concatenate([turned[:, k * 128 : k * 128 + 128] for k in range(8)], axis=0)
        turned = dot(turned, pick_ref[...])
        for k in range(16):
            for c in range(2):
                m = k % 2 * 2 + c
                piece = turned[k // 2 * 32 : k // 2 * 32 + 32, m * 128 : m * 128 + 128]
                wide_ref[part, 1, k, c * 32 : c * 32 + 32] = piece
    lane = lax.broadcasted_iota(jnp.int32, (1, 128), 1) // 32
    for g in range(8):
        classes = [class_ref[0, 0, g * 4 + t] for t in range(4)]
        for c in range(2):
            beta = jnp.full((1, 128), coupling_ref[classes[0], c])
            for t in range(1, 4):
                beta = jnp.where(lane == t, coupling_ref[classes[t], c], beta)
            row_ref[c : c + 1, g * 128 : g * 128 + 128] = beta
        for part in range(2):
            total = []
            for turned in range(2):
                for c in range(2):
                    own = [
                        wide_ref[part, turned, classes[t], c * 32 : c * 32 + 32] * own_ref[t, :, :128] for t in range(4)
                    ]
                    total.append((own[0] + own[1]) + (own[2] + own[3]))
            mx_ref[part, g, :32, :128] = total[0]
            mx_ref[part, g, :32, 128:] = -total[1]
            mx_ref[part, g, 32:, :128] = total[1]
            mx_ref[part, g, 32:, 128:] = total[0]
            my_ref[part, g, :32, :128] = total[2]
            my_ref[part, g, :32, 128:] = total[3]
            my_ref[part, g, 32:, :128] = -total[3]
            my_ref[part, g, 32:, 128:] = total[2]


def finish(
    in_ref, w3_ref, twist_ref, lens_ref, row_ref, mx_ref, my_ref, own_ref, fresh_any,
    out_ref, real_ref, mixed_ref, lensed_ref, rhs_ref, across_ref, fresh_ref, sem,
):
    copy = pltpu.make_async_copy(fresh_any, fresh_ref, sem)
    copy.start()
    lane = lane_of((8, 128))
    sides = [None, None]
    for m in range(4):
        pieces = in_ref[pl.ds(17 + SECOND * m, 8, stride=4 * SECOND), :]
        for side in range(2):
            piece = pltpu.roll(pieces, (32 * m - 32 * side) % 128, 1)
            sides[side] = piece if m == 0 else jnp.where(lane // 32 == m, piece, sides[side])
    side_lens = []
    for side in range(2):
        cos, sin = sincos(row_ref[2:3, :128] * (sides[side] - row_ref[3:4, :128]) * DEPTH_KM)
        side_lens.append((cos * NORM, sin * NORM))
    beside = jnp.concatenate(
        [jnp.broadcast_to(in_ref[SECOND * j + 16 : SECOND * j + 17], (8, 128)) for j in range(LAT)], axis=0
    )
    own = lane_of((256, 128)) % 32 // 4 == lax.broadcasted_iota(jnp.int32, (256, 128), 0) % 8
    turned = jnp.concatenate([line.T for line in both_tiles(in_ref, SECOND)], axis=0)
    mixed_ref[:256] = product(split(turned), (w3_ref[0], w3_ref[1]))
    mixed_ref[256:384] = product(split(jnp.where(own, beside, 0.0).T), (w3_ref[0], w3_ref[1]))
    halos = []
    for k1l in range(4):
        top = 256 + k1l * 32
        total = [
            (mixed_ref[top : top + 8, c] + mixed_ref[top + 8 : top + 16, c])
            + (mixed_ref[top + 16 : top + 24, c] + mixed_ref[top + 24 : top + 32, c])
            for c in (slice(0, 128), slice(128, 256))
        ]
        halos.append([part + pltpu.roll(part, 4, 0) for part in total])
    for block in range(5):
        values = []
        for k1 in range(8):
            top = k1 * 32 + block * 8
            if block < 4:
                value = (mixed_ref[top : top + 8, :128], mixed_ref[top : top + 8, 128:])
            else:
                value = halos[k1 % 4] if k1 < 4 else [pltpu.roll(part, 6, 0) for part in halos[k1 % 4]]
            if k1:
                value = cmul(value, (twist_ref[0, k1 : k1 + 1], twist_ref[1, k1 : k1 + 1]))
            values.append(value)
        for n1, value in enumerate(dft(values, 1)):
            lanes = slice(n1 * 128, n1 * 128 + 128)
            rows = slice(block * 8, block * 8 + 8)
            if block < 4:
                value = cmul(value, (lens_ref[0, rows, lanes], lens_ref[1, rows, lanes]))
                for c in range(2):
                    lensed_ref[c, 8 + block * 8 : 16 + block * 8, lanes] = value[c]
                continue
            for side, at in enumerate((7, 40)):
                pair = [value[c][side : side + 1] for c in range(2)]
                pair = cmul(pair, [side_lens[side][c][n1 : n1 + 1] for c in range(2)])
                for c in range(2):
                    lensed_ref[c, at : at + 1, lanes] = pair[c]
    for g in range(0, 8, 2):
        pair = []
        for lanes in (slice(g * 128, g * 128 + 128), slice(g * 128 + 128, g * 128 + 256)):
            beta = (row_ref[0:1, lanes], row_ref[1:2, lanes])
            mid = [lensed_ref[c, 8:40, lanes] for c in range(2)]
            diff = tuple(
                lensed_ref[c, 9:41, lanes] + lensed_ref[c, 7:39, lanes] - 2.0 * mid[c] for c in range(2)
            )
            more = cmul(diff, beta)
            pair.append([split(mid[c] + more[c]) for c in range(2)])
        rhs = [
            jnp.concatenate(
                [
                    jnp.concatenate([pieces[c][part] * own_ref[t, :, :128] for pieces in pair], axis=1)
                    for c in range(2)
                    for t in range(4)
                ],
                axis=0,
            )
            for part in range(2)
        ]
        left = [jnp.concatenate([mx_ref[part, g], mx_ref[part, g + 1]], axis=0) for part in range(2)]
        out = product(left, rhs)
        for c in range(2):
            across_ref[c, :, g * 128 : g * 128 + 128] = out[c * 32 : c * 32 + 32, :128]
            across_ref[c, :, g * 128 + 128 : g * 128 + 256] = out[64 + c * 32 : 96 + c * 32, 128:]
    lane = lax.broadcasted_iota(jnp.int32, (32, N), 1)
    diff = []
    for c in range(2):
        whole = across_ref[c]
        after = jnp.where(lane == N - 1, 0.0, pltpu.roll(whole, N - 1, 1))
        before = jnp.where(lane == 0, 0.0, pltpu.roll(whole, 1, 1))
        diff.append(after + before - 2.0 * whole)
    more = cmul(diff, (row_ref[0:1], row_ref[1:2]))
    for c in range(2):
        rhs_ref[c] = across_ref[c] + more[c]
    copy.wait()
    for g in range(8):
        lanes = slice(g * 128, g * 128 + 128)
        rhs = jnp.concatenate([rhs_ref[0, :, lanes], rhs_ref[1, :, lanes]], axis=1)
        tiles = [
            jnp.concatenate(
                [my_ref[part, g, c * 32 : c * 32 + 32] * own_ref[t] for c in range(2) for t in range(4)], axis=0
            )
            for part in range(2)
        ]
        out = product(split(rhs), tiles, NN)
        real_ref[:, lanes] = out[:, :128]
        last = row_ref[4:5, lanes] > 0.5
        for c in range(2):
            out_ref[c, :, lanes] = jnp.where(last, fresh_ref[c, :, lanes], out[:, c * 128 : c * 128 + 128])


def spread_y(field, slow, t):
    half = pltpu.VMEM((256, 256), jnp.bfloat16)
    scratch = [pltpu.VMEM((2, 32, N), jnp.float32), pltpu.VMEM((2, 8, 128), jnp.float32)]
    scratch += [pltpu.VMEM((2, 256, 256), jnp.bfloat16), pltpu.VMEM((16, N), jnp.float32), half, half]
    scratch += [pltpu.VMEM((2, 8, 128), jnp.float32), pltpu.SemaphoreType.DMA((5,))]
    args = [field, t["twist_y"], t["w1"], slow]
    return call(forward_y, [shape(LAT * FIRST, 128)], scratch, args, large=(0, 1, 2, 3))[0]


def prepared(freq, refslow, lat, last, classes, coupling, blocks, slow, t):
    half = jnp.bfloat16
    tables = [t["spread"], t["pick"], t["own"], t["x"], t["peers"], t["twist_x"]]
    args = [freq, refslow, lat, last, classes, coupling, blocks, slow, *tables]
    outs = [shape(2, 256, 128), shape(2, 32, N), shape(8, N)] + [shape(2, 8, 64, 256, dtype=half)] * 2
    outs += [jax.ShapeDtypeStruct(a.shape, a.dtype) for a in tables[2:]]
    scratch = [pltpu.VMEM((1024, 32), jnp.float32), pltpu.VMEM((32, N), jnp.float32), pltpu.VMEM((32, 128), half)]
    scratch += [pltpu.VMEM((128, 512), half), pltpu.VMEM((2, 2, 16, 64, 128), half), pltpu.SemaphoreType.DMA((8,))]
    phase, lens, rows, mx, my, own, x, peers, twist = call(
        prepare, outs, scratch, args, scalars=range(6), large=range(6, 14)
    )
    return [phase, x, peers, twist], [lens, rows, mx, my, own]


def continue_x(block, tabs):
    scratch = [pltpu.VMEM((256, 256), jnp.bfloat16)] * 2 + [pltpu.VMEM((192, N), jnp.bfloat16)]
    return call(along_x, [pltpu.VMEM((LAT * SECOND, 128), jnp.float32)], scratch, [block, *tabs])[0]


def correct(block, tabs, fresh, t):
    plane = pltpu.VMEM((2, 32, N), jnp.float32)
    scratch = [pltpu.VMEM((384, 256), jnp.float32), pltpu.VMEM((2, 48, N), jnp.float32)]
    scratch += [plane, plane, plane, pltpu.SemaphoreType.DMA]
    args = [block, t["w3"], t["twist_y"], *tabs, fresh]
    return call(finish, [shape(2, 32, N), shape(32, N)], scratch, args, large=(8,))


def exchange(block):
    blocks = block.reshape(LAT, 1, -1)
    return lax.all_to_all(blocks, "lat", split_axis=0, concat_axis=0, tiled=True).reshape(block.shape)


def after(value, *others):
    return lax.optimization_barrier((value, others))


def per_device(
    field, fresh, freq_index, ref_slowness, slowness, tile_classes, fd_blocks, fd_coupling, image
):
    t = tables()
    slow = slowness[0]
    block = spread_y(field.reshape(2, 32, N), slow, t)
    block, (blocks, slow) = after(block, fd_blocks.reshape(1024, 32), slow)
    received = exchange(block)
    lat = lax.axis_index("lat").reshape(1).astype(jnp.int32)
    count = lax.axis_size("depth")
    last = (lax.axis_index("depth") == count - 1).reshape(1).astype(jnp.int32)
    phase, tabs = prepared(freq_index, ref_slowness, lat, last, tile_classes, fd_coupling, blocks, slow, t)
    received, (phase, tabs) = after(received, phase, tabs)
    received = exchange(continue_x(received, phase))
    result, real = correct(received, tabs, fresh[0], t)
    next_field = lax.ppermute(result, "depth", [(i, (i + 1) % count) for i in range(count)])
    return next_field[None, None], image + real[None]


def solution(mesh):
    return jax.shard_map(
        per_device,
        mesh=mesh,
        in_specs=(
            P("depth", None, None, "lat", None),
            P(None, None, "lat", None),
            P("depth", None),
            P("depth"),
            P("depth", "lat", None),
            P("depth", "lat", None),
            P(),
            P(),
            P("depth", "lat", None),
        ),
        out_specs=(P("depth", None, None, "lat", None), P("depth", "lat", None)),
        check_vma=False,
    )
```
